32 devices in a mesh: wide: 8 (over y, x, core), narrow: 4 (over z).
Axes of the slice: x: 2, y: 2, z: 4, core: 2. Of those that a mesh axis runs over, the one named last changes fastest.
Arguments:
- x_input: float32 [8, 1024, 1152], P('wide', 'narrow'), may hold values from -6 to 6
- condition: float32 [8, 1152], P('wide'), may hold values from -6 to 6
- counts: int32 [8], P('wide'), may hold values from 1 to 1, as said below
- w_ada: bfloat16 [1152, 6912], P(None, 'narrow'), may hold values from -0.1875 to 0.1875
- b_ada: bfloat16 [6912], P('narrow'), may hold values from -3 to 3
- w_qkv: bfloat16 [1152, 3456], P('narrow'), may hold values from -0.1875 to 0.1875
- qv_bias: bfloat16 [2304], P('narrow'), may hold values from -3 to 3
- w_out: bfloat16 [1152, 1152], P('narrow'), may hold values from -1.5 to 1.5
- b_out: bfloat16 [1152], P('narrow'), may hold values from -3 to 3
- w_fc1: bfloat16 [1152, 4608], P('narrow'), may hold values from -0.1875 to 0.1875
- b_fc1: bfloat16 [4608], P('narrow'), may hold values from -3 to 3
- w_fc2: bfloat16 [4608, 1152], P('narrow'), may hold values from -0.09375 to 0.09375
- b_fc2: bfloat16 [1152], P('narrow'), may hold values from -3 to 3
- d_out: float32 [8, 1024, 1152], P('wide', 'narrow'), may hold values from -6 to 6
Outputs:
- result: float32 [8, 1024, 1152], P('wide', 'narrow')
- grad_input: float32 [8, 1024, 1152], P('wide', 'narrow')
- grad_condition: float32 [8, 1152], P('wide')
- grad_w_ada: float32 [1152, 6912], P(None, 'narrow')
- grad_b_ada: float32 [6912], P('narrow')
- grad_w_qkv: float32 [1152, 3456], P('narrow')
- grad_qv_bias: float32 [2304], P('narrow')
- grad_w_out: float32 [1152, 1152], P('narrow')
- grad_b_out: float32 [1152], P('narrow')
- grad_w_fc1: float32 [1152, 4608], P('narrow')
- grad_b_fc1: float32 [4608], P('narrow')
- grad_w_fc2: float32 [4608, 1152], P('narrow')
- grad_b_fc2: float32 [1152], P('narrow')
The draws below stay inside these ranges and needn't reach their ends.
Inputs may be any that keep to these rules, and one draw needn't show every extreme that they name: `counts`: each group holds 1 to 1 images, in its first slots; some group holds 1.
All inputs are finite; a program needn't handle non-finite values.
Results may differ from the reference program's by a relative error of at most 0.019.
Values may be sent and summed in bfloat16 or wider, within the bound.
No kernel may reach another device: no remote copies, remote signals or barrier semaphores. Data moves between devices by JAX's collectives and lax.ppermute only.
A program may use at most 256 MiB of HBM per device.

```python
import jax
import jax.numpy as jnp
from jax import lax

D = 1152
HEADS = 16
FF = 4608
IMG = 1024
SLOTS = 1
GROUPS = 8
SLOTS_ALL = 8


def draw_counts(key, part):
    first_key, second_key = jax.random.split(jax.random.fold_in(key, 11))
    base_counts = jax.random.randint(first_key, (GROUPS,), 1, SLOTS + 1)
    full_group = jax.random.randint(second_key, (), 0, GROUPS)
    return jnp.where(jnp.arange(GROUPS) == full_group, SLOTS, base_counts).astype(jnp.int32)


def level_of(own_key, dims, cuts, least, high):
    def one(position, blocks):
        steps = jax.random.uniform(jax.random.fold_in(jax.random.fold_in(own_key, 6), position), (blocks,), jnp.float32, least / len(cuts), high / len(cuts))
        return jnp.repeat(jnp.exp(steps), dims[position] // blocks).reshape((-1,) + (1,) * (len(dims) - position - 1))

    loudness = one(*cuts[0])
    for cut in cuts[1:]:
        loudness = loudness * one(*cut)
    return loudness


def scatter_about(rng, extent, width, reach, cuts=(), dtype=jnp.bfloat16):
    level = level_of(rng, extent, cuts, -0.22, 0.18) if cuts else 1.0
    drawn = jax.random.normal(rng, extent, jnp.float32) * width * level
    return jnp.minimum(jnp.maximum(drawn, -reach), reach).astype(dtype)


def setup_inputs(seed: int = 0) -> dict:
    splits = jax.random.split(jax.random.key(seed), 15)
    return {
        "x_input": scatter_about(splits[0], (SLOTS_ALL, IMG, D), 1.0, 6.0, ((0, 8), (1, 4)), jnp.float32),
        "condition": scatter_about(splits[1], (SLOTS_ALL, D), 1.0, 6.0, ((0, 8),), jnp.float32),
        "counts": draw_counts(jax.random.fold_in(splits[14], 71), 0),
        "w_ada": scatter_about(splits[3], (D, 6 * D), D ** -0.5, 0.1875, ((1, 4),)),
        "b_ada": scatter_about(splits[4], (6 * D,), 0.5, 3.0, ((0, 4),)),
        "w_qkv": scatter_about(splits[5], (D, 3 * D), D ** -0.5, 0.1875, ((0, 4),)),
        "qv_bias": scatter_about(splits[6], (2 * D,), 0.5, 3.0, ((0, 4),)),
        "w_out": scatter_about(splits[7], (D, D), (D // 64) ** -0.5, 1.5, ((0, 4),)),
        "b_out": scatter_about(splits[8], (D,), 0.5, 3.0, ((0, 4),)),
        "w_fc1": scatter_about(splits[9], (D, FF), D ** -0.5, 0.1875, ((0, 4),)),
        "b_fc1": scatter_about(splits[10], (FF,), 0.5, 3.0, ((0, 4),)),
        "w_fc2": scatter_about(splits[11], (FF, D), FF ** -0.5, 0.09375, ((0, 4),)),
        "b_fc2": scatter_about(splits[12], (D,), 0.5, 3.0, ((0, 4),)),
        "d_out": scatter_about(splits[13], (SLOTS_ALL, IMG, D), 1.0, 6.0, ((0, 8), (1, 4)), jnp.float32),
    }


@jax.custom_vjp
def low(v):
    return lax.optimization_barrier(v.astype(jnp.bfloat16)).astype(jnp.float32)

@jax.custom_vjp
def low_back(v):
    return v

def low_keep(v):
    return (low(v), None)

def low_pass(kept, grad):
    return (grad,)

def back_keep(v):
    return (v, None)

def back_low(kept, grad):
    return (low(grad),)
low.defvjp(low_keep, low_pass)
low_back.defvjp(back_keep, back_low)
highest = lax.Precision.HIGHEST

def normalize(rows_in):
    centered = rows_in - lax.optimization_barrier(jnp.mean(rows_in, axis=-1, keepdims=True))
    return centered * lax.rsqrt(lax.optimization_barrier(jnp.mean(centered * centered, axis=-1, keepdims=True)) + 1e-06)

def block(image_rows, condition_row, living_one, params):
    w_ada, b_ada, w_qkv, qv_bias, w_out, b_out, w_fc1, b_fc1, w_fc2, b_fc2 = params
    model_width = image_rows.shape[-1]
    head_count = HEADS
    head_size = model_width // head_count
    cond_low = low(jax.nn.silu(condition_row))
    modulation = low_back(jnp.dot(cond_low, w_ada, precision=highest) + b_ada)
    shift_one, scale_one, gate_one, shift_two, scale_two, gate_two = jnp.split(modulation, 6)
    first_in = low(normalize(image_rows) * (1.0 + scale_one) + shift_one)
    bias_three = jnp.concatenate([qv_bias[:model_width], jnp.zeros((model_width,), jnp.float32), qv_bias[model_width:]])
    projected = low(low_back(jnp.dot(first_in, w_qkv, precision=highest) + bias_three))
    queries = projected[:, :model_width].reshape(-1, head_count, head_size)
    key_rows = projected[:, model_width:2 * model_width].reshape(-1, head_count, head_size)
    value_rows = projected[:, 2 * model_width:].reshape(-1, head_count, head_size)
    scores = low_back(jnp.einsum('qhd,khd->hqk', queries, key_rows, precision=highest) * head_size ** (-0.5))
    softmax_rows = low(jax.nn.softmax(scores, axis=-1))
    mixed_rows = low(low_back(jnp.einsum('hqk,khd->qhd', softmax_rows, value_rows, precision=highest).reshape(-1, model_width)))
    branch_one = low_back(jnp.dot(mixed_rows, w_out, precision=highest) + b_out)
    middle = image_rows + gate_one * branch_one
    second = low(normalize(middle) * (1.0 + scale_two) + shift_two)
    hidden = low_back(jnp.dot(second, w_fc1, precision=highest) + b_fc1)
    active = low(jax.nn.gelu(hidden, approximate=True))
    branch_two = low_back(jnp.dot(active, w_fc2, precision=highest) + b_fc2)
    return living_one * (middle + gate_two * branch_two)

def reference(x_input, condition, counts, w_ada, b_ada, w_qkv, qv_bias, w_out, b_out, w_fc1, b_fc1, w_fc2, b_fc2, d_out):
    living = (jnp.arange(SLOTS)[None, :] < counts[:, None]).astype(jnp.float32).reshape(-1)
    params = tuple((weight.astype(jnp.float32) for weight in (w_ada, b_ada, w_qkv, qv_bias, w_out, b_out, w_fc1, b_fc1, w_fc2, b_fc2)))

    def forward(images, conditions, weights):

        def per_image(slot_item):
            return block(slot_item[0], slot_item[1], slot_item[2], weights)
        return lax.map(jax.checkpoint(per_image), (images, conditions, living))
    result, pull_back = jax.vjp(forward, x_input, condition, params)
    grad_input, grad_condition, weight_grads = pull_back(d_out)
    return (result, grad_input, grad_condition, weight_grads[0], weight_grads[1], weight_grads[2], weight_grads[3], weight_grads[4], weight_grads[5], weight_grads[6], weight_grads[7], weight_grads[8], weight_grads[9])
```

```python
import jax
import jax.numpy as jnp
from jax import lax
from jax.sharding import PartitionSpec as P

HEADS = 16
F32 = jnp.float32
BF16 = jnp.bfloat16


def dot(left, right, dims=((1,), (0,))):
    return lax.dot_general(left, right, (dims, ((), ())), preferred_element_type=F32)


def ring(block, step):
    n = lax.axis_size("narrow")
    return lax.ppermute(block, "narrow", [(i, (i + step) % n) for i in range(n)])


def flip(block, bit):
    w = lax.axis_size("wide")
    return lax.ppermute(block, "wide", [(i, i ^ bit) for i in range(w)])


def hop(block, bit):
    return flip(block.astype(BF16), bit).astype(F32)


def ring_gather(block):
    n = lax.axis_size("narrow")
    return [block] + [ring(block, step) for step in range(1, n)]


def place(blocks, index_of, axis=0):
    buffer = jnp.zeros((len(blocks),) + blocks[0].shape, blocks[0].dtype)
    for j, block in enumerate(blocks):
        buffer = lax.dynamic_update_index_in_dim(buffer, block, index_of(j), 0)
    return buffer


def link_bits():
    w = lax.axis_size("wide")
    return [1 << k for k in range(1, w.bit_length()) if (1 << k) < w]


def plane_gather(block):
    links = link_bits()
    got = {0: block}
    if len(links) == 2:
        u, v = links
        half = block.shape[0] // 2
        got[u] = flip(block, u)
        got[v] = flip(block, v)
        got[u | v] = jnp.concatenate([flip(got[u][:half], v), flip(got[v][half:], u)], axis=0)
    else:
        for bit in links:
            for r in list(got):
                got[r | bit] = flip(got[r], bit)
    for r in list(got):
        got[r | 1] = flip(got[r], 1)
    return [got[r] for r in range(len(got))]


def plane_reduce(blocks):
    links = link_bits()
    even = {r: blocks[r] + hop(blocks[r | 1], 1) for r in range(0, len(blocks), 2)}
    if len(links) == 2:
        u, v = links
        half = blocks[0].shape[0] // 2
        corner = even[u | v]
        by_v = jnp.concatenate([even[v][:half] + hop(corner[:half], u), even[v][half:]], axis=0)
        by_u = jnp.concatenate([even[u][:half], even[u][half:] + hop(corner[half:], v)], axis=0)
        return even[0] + hop(by_u, u) + hop(by_v, v)
    for bit in reversed(links):
        for r in [r for r in even if r & bit]:
            even[r ^ bit] = even[r ^ bit] + hop(even.pop(r), bit)
    return even[0]


def quad_gather(block):
    p = lax.axis_index("wide")
    two = flip(block, 2)
    parts = [block, flip(block, 1), two, flip(two, 1)]
    return place(parts, lambda r: (p & 3) ^ r)


def quad_reduce(terms):
    w = lax.axis_size("wide")
    p = lax.axis_index("wide")
    part = [lax.dynamic_index_in_dim(terms, (p & 3) ^ r, 1, keepdims=False) for r in range(4)]
    total = part[0] + hop(part[1], 1) + hop(part[2] + hop(part[3], 1), 2)
    bit = 4
    while bit < w:
        low = total.astype(BF16)
        total = low.astype(F32) + flip(low, bit).astype(F32)
        bit *= 2
    return total.astype(BF16)


def rows_mean(rows_in):
    return jnp.mean(rows_in, axis=-1, keepdims=True)


def norm_parts(rows_in):
    centered = rows_in - rows_mean(rows_in)
    inv = lax.rsqrt(rows_mean(centered * centered) + 1e-06)
    return centered * inv, inv


def norm_back(unit, inv, grad_unit):
    return inv * (grad_unit - rows_mean(grad_unit) - unit * rows_mean(grad_unit * unit))


def per_device(
    x_input,
    condition,
    counts,
    w_ada,
    b_ada,
    w_qkv,
    qv_bias,
    w_out,
    b_out,
    w_fc1,
    b_fc1,
    w_fc2,
    b_fc2,
    d_out,
):
    n = lax.axis_size("narrow")
    w = lax.axis_size("wide")
    z = lax.axis_index("narrow")
    p = lax.axis_index("wide")
    slot_count, tokens, width = x_input.shape
    x_rows = x_input.reshape(tokens, width)
    heads = HEADS // n
    head_size = width // HEADS
    score_scale = head_size ** (-0.5)
    shard = width // n
    sub = shard // 4
    hidden_dev = w_fc2.shape[0] // w
    hidden_all = n * hidden_dev
    cols = heads * head_size

    def ahead(j):
        return lax.rem(z + j, n)

    def behind(j):
        return lax.rem(z + n - j, n)

    living = (counts[0] > 0).astype(F32)

    cond_act, silu_pull = jax.vjp(jax.nn.silu, condition)
    cond_low = cond_act.astype(BF16)
    mod_part = dot(cond_low, w_ada)[0] + b_ada.astype(F32)
    unit_one, inv_one = norm_parts(x_rows)
    unit_low = unit_one.astype(BF16)
    small = jnp.concatenate([mod_part] + [v.astype(F32) for v in (qv_bias, b_out, b_fc1, b_fc2)])
    small_all = place(ring_gather(small), behind)
    ends = [0]
    for piece in (mod_part, qv_bias, b_out, b_fc1, b_fc2):
        ends.append(ends[-1] + piece.shape[0])
    modulation, qv_full, bout_full, bfc1_full, bfc2_full = [
        small_all[:, low:high].reshape(-1) for low, high in zip(ends[:-1], ends[1:])
    ]
    shift_one, scale_one, gate_one, shift_two, scale_two, gate_two = [
        modulation[None, k * width : (k + 1) * width] for k in range(6)
    ]

    unit_blocks = ring_gather(unit_low)

    qkv_mine = lax.dynamic_slice_in_dim(w_qkv, (p & 3) * sub, sub, 0)
    qkv_to = qkv_mine.reshape(sub, 3, n, cols).transpose(2, 0, 1, 3).reshape(n, sub, 3 * cols)
    qkv_got = [
        ring(lax.dynamic_index_in_dim(qkv_to, ahead(j), 0, keepdims=False), j) if j else
        lax.dynamic_index_in_dim(qkv_to, z, 0, keepdims=False)
        for j in range(n)
    ]
    qkv_cols = quad_gather(place(qkv_got, behind)).transpose(1, 0, 2, 3).reshape(width, 3 * cols)

    out_mine = lax.dynamic_slice_in_dim(w_out, (p & 3) * sub, sub, 0)
    out_blocks = ring_gather(out_mine)
    out_stack = jnp.stack([out_blocks[(n - j) % n] for j in range(n)])
    out_cat = quad_gather(out_stack).transpose(1, 0, 2, 3).reshape(width, width)

    fc1_mine = lax.dynamic_index_in_dim(
        w_fc1.reshape(shard, n, w, hidden_dev), p, 2, keepdims=False
    ).reshape(shard, hidden_all)
    fc1_dev = place(ring_gather(fc1_mine), behind).reshape(width, hidden_all)
    fc2_mine = lax.dynamic_slice_in_dim(w_fc2, p * hidden_dev, hidden_dev, 0)
    fc2_dev = place(ring_gather(fc2_mine), behind).reshape(hidden_all, width)
    bfc1_dev = lax.dynamic_index_in_dim(bfc1_full.reshape(n, w, hidden_dev), p, 1, keepdims=False)
    bfc1_dev = bfc1_dev.reshape(1, hidden_all)

    first_all = jnp.concatenate(
        [(b.astype(F32) * (1.0 + scale_one) + shift_one).astype(BF16) for b in unit_blocks], axis=0
    )
    qv_two = qv_full.reshape(2, n, cols)
    q_bias = lax.dynamic_index_in_dim(qv_two[0], z, 0, keepdims=True)
    v_bias = lax.dynamic_index_in_dim(qv_two[1], z, 0, keepdims=True)
    bias_three = jnp.concatenate([q_bias, jnp.zeros_like(q_bias), v_bias], axis=1)
    projected = (dot(first_all, qkv_cols) + bias_three).astype(BF16)
    image = n * tokens
    queries = projected[:, :cols].reshape(image, heads, head_size)
    keys = projected[:, cols : 2 * cols].reshape(image, heads, head_size)
    values = projected[:, 2 * cols :].reshape(image, heads, head_size)
    scores = jnp.einsum("qhd,khd->hqk", queries, keys, preferred_element_type=F32) * score_scale
    row_max = jnp.max(scores, axis=-1, keepdims=True)
    exponent = jnp.exp(scores - row_max)
    row_total = jnp.sum(exponent, axis=-1, keepdims=True)
    lse = row_max + jnp.log(row_total)
    attention = (exponent / row_total).astype(BF16)
    mixed = jnp.einsum("hqk,khd->qhd", attention, values, preferred_element_type=F32)
    mixed = mixed.astype(BF16).reshape(n, tokens, cols)
    mixed_cat = jnp.concatenate(
        [mixed[0]] + [ring(mixed[j], n - j) for j in range(1, n)], axis=1
    )

    branch_one = dot(mixed_cat, out_cat) + bout_full[None]
    middle = x_rows + gate_one * branch_one
    unit_two, inv_two = norm_parts(middle)
    second_low = (unit_two * (1.0 + scale_two) + shift_two).astype(BF16)

    grad_out = living * d_out.reshape(tokens, width)
    grad_two = (gate_two * grad_out).astype(BF16)
    two_all = jnp.concatenate(plane_gather(grad_two), axis=0)
    second_all = jnp.concatenate(plane_gather(second_low), axis=0)
    hidden_pre = dot(second_all, fc1_dev) + bfc1_dev
    active_pre, gelu_pull = jax.vjp(lambda v: jax.nn.gelu(v, approximate=True), hidden_pre)
    active = active_pre.astype(BF16)
    grad_active = dot(two_all, fc2_dev, ((1,), (1,)))
    grad_hidden = gelu_pull(grad_active)[0].astype(BF16)
    second_terms = dot(grad_hidden, fc1_dev, ((1,), (1,))).reshape(w, tokens, width)
    grad_second = plane_reduce([second_terms[r] for r in range(w)])
    two_terms = dot(active, fc2_dev).reshape(w, tokens, width)
    branch_two = plane_reduce([two_terms[r] for r in range(w)]) + bfc2_full[None]
    result = living * (middle + gate_two * branch_two)
    grad_gate_two = jnp.sum(grad_out * branch_two, axis=0)

    def narrow_sum(terms):
        low = terms.astype(BF16)
        got = [lax.dynamic_index_in_dim(low, z, 0, keepdims=False)]
        got += [
            ring(lax.dynamic_index_in_dim(low, ahead(j), 0, keepdims=False), j) for j in range(1, n)
        ]
        return sum(g.astype(F32) for g in got)

    wfc2_own = narrow_sum(dot(active, two_all, ((0,), (0,))).reshape(n, hidden_dev, width))
    grad_wfc2 = place(plane_gather(wfc2_own.astype(BF16)), lambda r: p ^ r)
    grad_wfc2 = grad_wfc2.reshape(w * hidden_dev, width).astype(F32)
    wfc1_own = narrow_sum(dot(second_all, grad_hidden, ((0,), (0,))).reshape(n, shard, hidden_all))
    grad_wfc1 = place(plane_gather(wfc1_own.astype(BF16)), lambda r: p ^ r)
    grad_wfc1 = grad_wfc1.reshape(w, shard, n, hidden_dev).transpose(1, 2, 0, 3)
    grad_wfc1 = grad_wfc1.reshape(shard, n * w * hidden_dev).astype(F32)
    bfc1_terms = jnp.sum(grad_hidden.astype(F32), axis=0)
    bfc2_terms = jnp.sum(grad_two.astype(F32), axis=0)

    grad_shift_two = jnp.sum(grad_second, axis=0)
    grad_scale_two = jnp.sum(grad_second * unit_two, axis=0)
    grad_middle = grad_out + norm_back(unit_two, inv_two, grad_second * (1.0 + scale_two))
    grad_one = (gate_one * grad_middle).astype(BF16)
    grad_gate_one = jnp.sum(grad_middle * branch_one, axis=0)
    bout_terms = jnp.sum(grad_one.astype(F32), axis=0)
    grad_mixed_cat = dot(grad_one, out_cat, ((1,), (1,))).astype(BF16).reshape(tokens, n, cols)
    grad_mixed = jnp.concatenate(
        [grad_mixed_cat[:, 0]] + [ring(grad_mixed_cat[:, j], j) for j in range(1, n)], axis=0
    ).reshape(image, heads, head_size)
    wout_terms = dot(mixed_cat, grad_one, ((0,), (0,))).reshape(n, 4, sub, width)
    wout_quad = quad_reduce(wout_terms)
    wout_own = wout_quad[0].astype(F32) + sum(
        ring(wout_quad[j], j).astype(F32) for j in range(1, n)
    )
    grad_wout = quad_gather(wout_own.astype(BF16)).reshape(shard, width).astype(F32)

    scores = jnp.einsum("qhd,khd->hqk", queries, keys, preferred_element_type=F32) * score_scale
    weights = jnp.exp(scores - lse)
    grad_attention = jnp.einsum("qhd,khd->hqk", grad_mixed, values, preferred_element_type=F32)
    delta = jnp.sum(weights * grad_attention, axis=-1, keepdims=True)
    grad_scores = (weights * (grad_attention - delta)).astype(BF16)
    grad_queries = (
        jnp.einsum("hqk,khd->qhd", grad_scores, keys, preferred_element_type=F32) * score_scale
    )
    grad_keys = (
        jnp.einsum("hqk,qhd->khd", grad_scores, queries, preferred_element_type=F32) * score_scale
    )
    grad_values = jnp.einsum(
        "hqk,qhd->khd", weights.astype(BF16), grad_mixed, preferred_element_type=F32
    )
    grad_projected = jnp.concatenate(
        [g.astype(BF16).reshape(image, cols) for g in (grad_queries, grad_keys, grad_values)], axis=1
    )
    first_terms = dot(grad_projected, qkv_cols, ((1,), (1,)))
    unit_all = jnp.concatenate(unit_blocks, axis=0)
    grad_shift_one = jnp.sum(first_terms, axis=0)
    grad_scale_one = jnp.sum(first_terms * unit_all.astype(F32), axis=0)
    first_low = first_terms.astype(BF16).reshape(n, tokens, width)
    grad_first = first_low[0].astype(F32) + sum(
        ring(first_low[j], n - j).astype(F32) for j in range(1, n)
    )
    grad_input = grad_middle + norm_back(unit_one, inv_one, grad_first * (1.0 + scale_one))

    wqkv_terms = dot(first_all, grad_projected, ((0,), (0,))).reshape(n, 4, sub, 3 * cols)
    wqkv_quad = quad_reduce(wqkv_terms)
    wqkv_got = [lax.dynamic_index_in_dim(wqkv_quad, z, 0, keepdims=False)] + [
        ring(lax.dynamic_index_in_dim(wqkv_quad, ahead(j), 0, keepdims=False), j)
        for j in range(1, n)
    ]
    wqkv_all = quad_gather(place(wqkv_got, behind))
    grad_wqkv = wqkv_all.reshape(4, n, sub, 3, cols).transpose(0, 2, 3, 1, 4)
    grad_wqkv = grad_wqkv.reshape(shard, 3 * width).astype(F32)
    projected_sums = jnp.sum(grad_projected.astype(F32), axis=0).reshape(3, cols)

    mod_terms = jnp.concatenate(
        [grad_shift_one, grad_scale_one, grad_gate_one, grad_shift_two, grad_scale_two, grad_gate_two]
    ).reshape(n, -1)
    qv_terms = jnp.zeros((2, n, cols), F32)
    qv_terms = lax.dynamic_update_slice(
        qv_terms, jnp.stack([projected_sums[0], projected_sums[2]])[:, None], (0, z, 0)
    )
    bfc1_wide = lax.dynamic_update_slice(
        jnp.zeros((n, w, hidden_dev), F32), bfc1_terms.reshape(n, 1, hidden_dev), (0, p, 0)
    )
    small_terms = jnp.concatenate(
        [
            mod_terms,
            qv_terms.reshape(n, -1),
            bout_terms.reshape(n, -1),
            bfc1_wide.reshape(n, -1),
            bfc2_terms.reshape(n, -1),
        ],
        axis=1,
    )
    small_own = lax.dynamic_index_in_dim(small_terms, z, 0, keepdims=False) + sum(
        ring(lax.dynamic_index_in_dim(small_terms, ahead(j), 0, keepdims=False), j)
        for j in range(1, n)
    )
    mod_size = mod_terms.shape[1]
    mod_low = small_own[:mod_size].astype(BF16)
    cond_part = dot(mod_low[None], w_ada, ((1,), (1,)))
    cond_total = cond_part + sum(ring(cond_part, j) for j in range(1, n))
    grad_condition = silu_pull(cond_total)[0]
    shared = jnp.concatenate([small_own, cond_act[0]])[None]
    bits = [1] + link_bits()
    for bit in bits:
        shared = jnp.concatenate([shared, flip(shared, bit)], axis=0)
    order = jnp.arange(w) ^ p
    shared = shared[order]
    mod_rows = shared[:, :mod_size].astype(BF16)
    cond_rows = shared[:, small_own.shape[0] :].astype(BF16)
    grad_wada = dot(cond_rows, mod_rows, ((0,), (0,)))
    grad_bada = jnp.sum(mod_rows.astype(F32), axis=0)
    bias_sums = jnp.sum(shared[:, mod_size : small_own.shape[0]], axis=0)
    ends = [0]
    for piece in (qv_bias, b_out, b_fc1, b_fc2):
        ends.append(ends[-1] + piece.shape[0])
    grad_qv, grad_bout, grad_bfc1, grad_bfc2 = [
        bias_sums[low:high] for low, high in zip(ends[:-1], ends[1:])
    ]
    return (
        result[None],
        grad_input[None],
        grad_condition,
        grad_wada,
        grad_bada,
        grad_wqkv,
        grad_qv,
        grad_wout,
        grad_bout,
        grad_wfc1,
        grad_bfc1,
        grad_wfc2,
        grad_bfc2,
    )


def solution(mesh):
    in_specs = (
        P("wide", "narrow", None),
        P("wide", None),
        P("wide"),
        P(None, "narrow"),
        P("narrow"),
        P("narrow", None),
        P("narrow"),
        P("narrow", None),
        P("narrow"),
        P("narrow", None),
        P("narrow"),
        P("narrow", None),
        P("narrow"),
        P("wide", "narrow", None),
    )
    out_specs = (
        P("wide", "narrow", None),
        P("wide", "narrow", None),
        P("wide", None),
        P(None, "narrow"),
        P("narrow"),
        P("narrow", None),
        P("narrow"),
        P("narrow", None),
        P("narrow"),
        P("narrow", None),
        P("narrow"),
        P("narrow", None),
        P("narrow"),
    )
    return jax.shard_map(
        per_device, mesh=mesh, in_specs=in_specs, out_specs=out_specs, check_vma=False
    )
```

```python
import functools
import math

import jax
import jax.numpy as jnp
from jax import lax
from jax.experimental import pallas as pl
from jax.experimental.pallas import tpu as pltpu
from jax.sharding import Mesh
from jax.sharding import PartitionSpec as P

HEADS = 16
WIDE = ("chip", "core")
F32 = jnp.float32
BF16 = jnp.bfloat16
LANES = 128
ROOT = math.sqrt(2 / math.pi)


def dot(left, right, dims=((1,), (0,))):
    return lax.dot_general(left, right, (dims, ((), ())), preferred_element_type=F32)


def flip(block, axis, bit):
    size = lax.axis_size(axis)
    return lax.ppermute(block, axis, [(i, i ^ bit) for i in range(size)])


def exchange(blocks, axis):
    return lax.all_to_all(blocks, axis, 0, 0, tiled=False)


def share(block, axis):
    return exchange(jnp.broadcast_to(block[None], (lax.axis_size(axis),) + block.shape), axis)


def ring(block, step):
    n = lax.axis_size("narrow")
    return lax.ppermute(block, "narrow", [(i, (i + step) % n) for i in range(n)])


def together(*values):
    return lax.optimization_barrier(values)


def add_up(blocks):
    return sum(blocks[i].astype(F32) for i in range(blocks.shape[0]))


def place(blocks, index_of):
    buffer = jnp.zeros((len(blocks),) + blocks[0].shape, blocks[0].dtype)
    for j, block in enumerate(blocks):
        buffer = lax.dynamic_update_index_in_dim(buffer, block, index_of(j), 0)
    return buffer


def quad_index(r):
    chip = lax.axis_index("chip")
    core = lax.axis_index("core")
    return 2 * ((chip & 1) ^ (r >> 1)) + (core ^ (r & 1))


def quad_gather(block):
    two = flip(block, "chip", 1)
    pair = flip(jnp.stack([block, two]), "core", 1)
    return place([block, pair[0], two, pair[1]], quad_index)


def ring_sum(terms):
    n = lax.axis_size("narrow")
    z = lax.axis_index("narrow")
    total = lax.dynamic_index_in_dim(terms, z, 0, keepdims=False)
    for j in range(1, n):
        total += ring(lax.dynamic_index_in_dim(terms, lax.rem(z + j, n), 0, keepdims=False), j)
    return total


def ring_gather(block):
    n = lax.axis_size("narrow")
    z = lax.axis_index("narrow")
    blocks = [block] + [ring(block, j) for j in range(1, n)]
    return place(blocks, lambda j: lax.rem(z + n - j, n))


def plane_rows(row):
    chips = lax.axis_size("chip")
    p = 2 * lax.axis_index("chip") + lax.axis_index("core")
    own = jnp.stack([row] + [flip(row, "chip", r) for r in range(1, chips)])
    both = jnp.stack([own, flip(own, "core", 1)], axis=1).reshape((2 * chips,) + row.shape)
    return both[jnp.arange(2 * chips) ^ p]


def plane_share(block):
    own = share(block, "chip")
    return own, flip(own, "core", 1)


def chip_sum(terms):
    chip = lax.axis_index("chip")
    total = lax.dynamic_index_in_dim(terms, chip, 0, keepdims=False).astype(F32)
    for r in range(1, lax.axis_size("chip")):
        term = lax.dynamic_index_in_dim(terms, chip ^ r, 0, keepdims=False)
        total += flip(term, "chip", r).astype(F32)
    return total


def core_add(own, other):
    return (own.astype(F32) + flip(other, "core", 1).astype(F32)).astype(BF16)


def call(kernel, args, outs, scratch=(), scalars=0, name=None, micros=1):
    vmem = pl.BlockSpec(memory_space=pltpu.VMEM)
    smem = pl.BlockSpec(memory_space=pltpu.SMEM)
    return pl.pallas_call(
        kernel,
        out_shape=tuple(jax.ShapeDtypeStruct(shape, dtype) for shape, dtype in outs),
        in_specs=[smem if i < scalars else vmem for i in range(len(args))],
        out_specs=tuple(vmem for _ in outs),
        scratch_shapes=[pltpu.VMEM(shape, dtype) for shape, dtype in scratch],
        compiler_params=pltpu.CompilerParams(vmem_limit_bytes=56 << 20),
        cost_estimate=pl.CostEstimate(
            flops=1000000000 * micros, bytes_accessed=3000000 * micros, transcendentals=0
        ),
        name=name,
    )(*args)


def pack_kernel(n, w, p_ref, fc1_ref, fc2_ref, pack_ref):
    shard = fc1_ref.shape[0]
    rows = fc2_ref.shape[0] // w
    full = fc2_ref.shape[0]
    for q in range(w):

        @pl.when(p_ref[0] == q)
        def _(q=q):
            pack_ref[:rows] = fc2_ref[q * rows : (q + 1) * rows]
            pieces = [
                fc1_ref[part : part + rows, a * full + q * rows : a * full + (q + 1) * rows]
                for part in range(0, shard, rows)
                for a in range(n)
            ]
            pack_ref[rows:] = jnp.concatenate(pieces, axis=1)


def qkv_kernel(n, place_ref, w_ref, out_ref):
    sub = out_ref.shape[1]
    cols = out_ref.shape[2] // 3
    width = w_ref.shape[1] // 3
    for q in range(w_ref.shape[0] // sub):

        @pl.when(place_ref[0] == q)
        def _(q=q):
            for a in range(n):
                out_ref[a] = jnp.concatenate(
                    [
                        w_ref[q * sub : (q + 1) * sub, t * width + a * cols : t * width + (a + 1) * cols]
                        for t in range(3)
                    ],
                    axis=1,
                )


def attend_kernel(
    n, heads, scale, unit_ref, mod_ref, w_ref, bias_ref, mixed_ref, proj_ref, lse_ref, wide_ref
):
    image, width = unit_ref.shape
    tokens = image // n
    cols = w_ref.shape[1] // 3
    size = cols // heads
    pad = jnp.zeros((width, LANES - size), BF16)
    pad_row = jnp.zeros((1, LANES - size), F32)
    bias = []
    for t in range(3 * heads):
        wide_ref[:, t * LANES : (t + 1) * LANES] = jnp.concatenate(
            [w_ref[:, t * size : (t + 1) * size], pad], axis=1
        )
        bias += [bias_ref[:, t * size : (t + 1) * size], pad_row]
    bias = jnp.concatenate(bias, axis=1)
    gain = 1.0 + mod_ref[1:2]
    shift = mod_ref[0:1]

    def project(i, carry):
        rows = pl.ds(pl.multiple_of(i * tokens, tokens), tokens)
        first = (unit_ref[rows].astype(F32) * gain + shift).astype(BF16)
        proj_ref[rows] = (dot(first, wide_ref[...]) + bias).astype(BF16)
        return carry

    lax.fori_loop(0, n, project, 0)
    for h in range(heads):
        keys = proj_ref[:, (heads + h) * LANES : (heads + h + 1) * LANES]
        values = proj_ref[:, (2 * heads + h) * LANES : (2 * heads + h + 1) * LANES]
        values_t = values.T

        def block(i, carry, h=h, keys=keys, values_t=values_t):
            rows = pl.ds(pl.multiple_of(i * tokens, tokens), tokens)
            queries = proj_ref[rows, h * LANES : (h + 1) * LANES]
            scores = dot(keys, queries, ((1,), (1,)))
            top = jnp.max(scores, axis=0, keepdims=True)
            grown = jnp.exp((scores - top) * scale)
            total = jnp.sum(grown, axis=0, keepdims=True)
            mixed = dot(values_t, grown.astype(BF16)) / total
            mixed_ref[i, :, h * size : (h + 1) * size] = mixed.T[:, :size].astype(BF16)
            lse_ref[h : h + 1, rows] = top * scale + jnp.log(total)
            return carry

        lax.fori_loop(0, n, block, 0)


def attend_back_kernel(
    n,
    heads,
    scale,
    core_ref,
    proj_ref,
    lse_ref,
    grad_ref,
    mixed_ref,
    unit_ref,
    mod_ref,
    *rest,
):
    terms_own_ref, terms_other_ref, grad_proj, proj_sums_ref, grad_wide, delta_ref, first_low = rest[:7]
    terms, query_acc, terms_low = rest[7:]
    image, width = unit_ref.shape
    tokens = image // n
    cols = grad_ref.shape[2]
    size = cols // heads
    pad = jnp.zeros((tokens, LANES - size), BF16)
    ones = jnp.ones((8, LANES), F32)
    gain = 1.0 + mod_ref[1:2]
    shift = mod_ref[0:1]

    def prepare(i, carry):
        rows = pl.ds(pl.multiple_of(i * tokens, tokens), tokens)
        for h in range(heads):
            grad = jnp.concatenate([grad_ref[i, :, h * size : (h + 1) * size], pad], axis=1)
            mixed = jnp.concatenate([mixed_ref[i, :, h * size : (h + 1) * size], pad], axis=1)
            grad_wide[rows, h * LANES : (h + 1) * LANES] = grad
            both = grad.astype(F32) * mixed.astype(F32)
            delta = lax.dot_general(
                ones, both, (((1,), (1,)), ((), ())),
                preferred_element_type=F32, precision=lax.Precision.HIGHEST,
            )
            delta_ref[h : h + 1, rows] = delta[0:1]
        first_low[rows] = (unit_ref[rows].astype(F32) * gain + shift).astype(BF16)
        return carry

    lax.fori_loop(0, n, prepare, 0)
    for h in range(heads):
        q_at = slice(h * LANES, (h + 1) * LANES)
        k_at = slice((heads + h) * LANES, (heads + h + 1) * LANES)
        v_at = slice((2 * heads + h) * LANES, (2 * heads + h + 1) * LANES)
        query_acc[...] = jnp.zeros_like(query_acc)

        def block(j, carry, h=h, q_at=q_at, k_at=k_at, v_at=v_at):
            rows = pl.ds(pl.multiple_of(j * tokens, tokens), tokens)
            keys = proj_ref[rows, k_at]
            values = proj_ref[rows, v_at]
            queries = proj_ref[:, q_at]
            grads = grad_wide[:, q_at]
            weights = jnp.exp(dot(keys, queries, ((1,), (1,))) * scale - lse_ref[h : h + 1])
            grad_weights = dot(values, grads, ((1,), (1,)))
            grad_scores = (weights * (grad_weights - delta_ref[h : h + 1])).astype(BF16)
            grad_proj[rows, v_at] = dot(weights.astype(BF16), grads).astype(BF16)
            grad_proj[rows, k_at] = (dot(grad_scores, queries) * scale).astype(BF16)
            query_acc[...] += dot(keys.T, grad_scores)
            return carry

        lax.fori_loop(0, n, block, 0)
        grad_proj[:, q_at] = (query_acc[...] * scale).T.astype(BF16)

    proj_sums_ref[...] = jnp.zeros_like(proj_sums_ref)
    for i in range(n):
        block = grad_proj[i * tokens : (i + 1) * tokens].astype(F32)
        proj_sums_ref[0:1] += jnp.sum(block, axis=0, keepdims=True)
    for t in range(3):
        part = dot(
            first_low[...], grad_proj[:, t * heads * LANES : (t + 1) * heads * LANES], ((0,), (0,))
        )
        terms[:, t * cols : (t + 1) * cols] = jnp.concatenate(
            [part[:, h * LANES : h * LANES + size] for h in range(heads)], axis=1
        )
    to_pieces(terms, terms_low, n)
    terms_own_ref[...] = terms_low[core_ref[0]]
    terms_other_ref[...] = terms_low[1 - core_ref[0]]


def to_pieces(terms, low, n):
    _, chips, _, padded, columns = low.shape
    shard = terms.shape[0] // n
    piece = shard // (2 * chips)
    for a in range(n):
        for q in range(2 * chips):
            at = a * shard + q * piece
            block = terms[at : at + piece].astype(BF16)
            if padded > piece:
                block = jnp.concatenate([block, jnp.zeros((padded - piece, columns), BF16)], axis=0)
            low[q % 2, q // 2, a] = block


def wout_kernel(n, core_ref, mixed_ref, grad_ref, own_ref, other_ref, terms, low):
    step = grad_ref.shape[1] // 3
    for t in range(3):
        lanes = slice(t * step, (t + 1) * step)
        terms[:, lanes] = dot(mixed_ref[...], grad_ref[:, lanes], ((0,), (0,)))
    to_pieces(terms, low, n)
    own_ref[...] = low[core_ref[0]]
    other_ref[...] = low[1 - core_ref[0]]


def first_kernel(n, grad_proj, wide_ref, unit_ref, first_ref, sums_ref):
    tokens = unit_ref.shape[0] // n
    sums_ref[...] = jnp.zeros_like(sums_ref)

    def block(i, carry):
        rows = pl.ds(pl.multiple_of(i * tokens, tokens), tokens)
        grad = dot(grad_proj[rows], wide_ref[...], ((1,), (1,)))
        sums_ref[0:1] += jnp.sum(grad, axis=0, keepdims=True)
        sums_ref[1:2] += jnp.sum(grad * unit_ref[rows].astype(F32), axis=0, keepdims=True)
        first_ref[i] = grad.astype(BF16)
        return carry

    lax.fori_loop(0, n, block, 0)


def mlp_kernel(
    n,
    own_ref,
    other_ref,
    two_own_ref,
    two_other_ref,
    pack_ref,
    bias_ref,
    second_own_ref,
    second_other_ref,
    two_sum_own_ref,
    two_sum_other_ref,
    grad_ref,
    bias_grad_ref,
    fc1,
    fc2,
    active_all,
    hidden_all,
    grad_fc1,
):
    chips, tokens, width = own_ref.shape
    rows = pack_ref.shape[1] // 2
    units = n * rows
    halves = width // units
    for a in range(n):
        fc2[a * rows : (a + 1) * rows] = pack_ref[a, :rows]
        for part in range(halves):
            at = (a * halves + part) * rows
            fc1[at : at + rows] = pack_ref[a, rows:, part * units : (part + 1) * units]
    bias_grad_ref[...] = jnp.zeros_like(bias_grad_ref)
    sides = (
        (own_ref, two_own_ref, second_own_ref, two_sum_own_ref),
        (other_ref, two_other_ref, second_other_ref, two_sum_other_ref),
    )
    for side, refs in enumerate(sides):

        def block(i, carry, side=side, refs=refs):
            x_ref, g_ref, second_ref, two_ref = refs
            at = pl.ds(pl.multiple_of((side * chips + i) * tokens, tokens), tokens)
            hidden = dot(x_ref[i], fc1[...]) + bias_ref[...]
            square = hidden * hidden
            inner = ROOT * (hidden + 0.044715 * square * hidden)
            bend = jnp.tanh(inner)
            half = 0.5 * (1.0 + bend)
            active = (hidden * half).astype(BF16)
            slope = half + 0.5 * hidden * (1.0 - bend * bend) * (ROOT * (1.0 + 3 * 0.044715 * square))
            grad = (dot(g_ref[i], fc2[...], ((1,), (1,))) * slope).astype(BF16)
            active_all[at] = active
            hidden_all[at] = grad
            second_ref[i] = dot(grad, fc1[...], ((1,), (1,))).astype(BF16)
            two_ref[i] = dot(active, fc2[...]).astype(BF16)
            bias_grad_ref[0:1] += jnp.sum(grad.astype(F32), axis=0, keepdims=True)
            return carry

        lax.fori_loop(0, chips, block, 0)
    step = width // 3
    half_rows = chips * tokens
    for t in range(3):
        lanes = slice(t * step, (t + 1) * step)
        part = dot(
            active_all[:half_rows], two_own_ref[:, :, lanes].reshape(half_rows, step), ((0,), (0,))
        ) + dot(
            active_all[half_rows:], two_other_ref[:, :, lanes].reshape(half_rows, step), ((0,), (0,))
        )
        for a in range(n):
            grad_ref[a, :rows, lanes] = part[a * rows : (a + 1) * rows].astype(BF16)
        grad_fc1[lanes] = dot(
            own_ref[:, :, lanes].reshape(half_rows, step), hidden_all[:half_rows], ((0,), (0,))
        ) + dot(
            other_ref[:, :, lanes].reshape(half_rows, step), hidden_all[half_rows:], ((0,), (0,))
        )
    for a in range(n):
        grad_ref[a, rows:] = jnp.concatenate(
            [
                grad_fc1[(a * halves + part) * rows : (a * halves + part + 1) * rows].astype(BF16)
                for part in range(halves)
            ],
            axis=1,
        )


def unpack_kernel(n, got_ref, fc1_ref, fc2_ref):
    w, _, width = got_ref.shape
    rows = got_ref.shape[1] // 2
    units = n * rows
    full = w * rows
    for q in range(w):
        fc2_ref[q * rows : (q + 1) * rows] = got_ref[q, :rows].astype(F32)
    for part in range(width // units):
        for a in range(n):
            at = part * units + a * rows
            fc1_ref[part * rows : (part + 1) * rows, a * full : (a + 1) * full] = jnp.concatenate(
                [got_ref[q, rows:, at : at + rows].astype(F32) for q in range(w)], axis=1
            )


def unpack_qkv_kernel(n, core_ref, own_ref, other_ref, out_ref):
    chips = own_ref.shape[0]
    piece = out_ref.shape[0] // (2 * chips)
    cols = own_ref.shape[3] // 3
    for core in range(2):

        @pl.when(core_ref[0] == core)
        def _(core=core):
            for q in range(2 * chips):
                got_ref = own_ref if q % 2 == core else other_ref
                out_ref[q * piece : (q + 1) * piece] = jnp.concatenate(
                    [
                        got_ref[q // 2, a, :piece, t * cols : (t + 1) * cols].astype(F32)
                        for t in range(3)
                        for a in range(n)
                    ],
                    axis=1,
                )


def rows_mean(rows_in):
    return jnp.mean(rows_in, axis=-1, keepdims=True)


def norm_parts(rows_in):
    centered = rows_in - rows_mean(rows_in)
    inv = lax.rsqrt(rows_mean(centered * centered) + 1e-06)
    return centered * inv, inv


def norm_back(unit, inv, grad_unit):
    return inv * (grad_unit - rows_mean(grad_unit) - unit * rows_mean(grad_unit * unit))


def per_device(
    x_input,
    condition,
    counts,
    w_ada,
    b_ada,
    w_qkv,
    qv_bias,
    w_out,
    b_out,
    w_fc1,
    b_fc1,
    w_fc2,
    b_fc2,
    d_out,
):
    n = lax.axis_size("narrow")
    chips = lax.axis_size("chip")
    w = 2 * chips
    z = lax.axis_index("narrow")
    p = 2 * lax.axis_index("chip") + lax.axis_index("core")
    plane = ("chip", "core")
    slot_count, tokens, width = x_input.shape
    x_rows = x_input.reshape(tokens, width)
    heads = HEADS // n
    head_size = width // HEADS
    score_scale = head_size ** (-0.5)
    shard = width // n
    sub = shard // 4
    hidden_dev = w_fc2.shape[0] // w
    hidden_all = n * hidden_dev
    cols = heads * head_size
    image = n * tokens

    living = (counts[0] > 0).astype(F32)

    quad_at = jnp.asarray(quad_index(0), jnp.int32).reshape(1)
    (qkv_to,) = call(
        functools.partial(qkv_kernel, n),
        (quad_at, w_qkv),
        [((n, sub, 3 * cols), BF16)],
        scalars=1,
        name="qkv_to",
        micros=3,
    )

    cond_act, silu_pull = jax.vjp(jax.nn.silu, condition)
    cond_low = cond_act.astype(BF16)
    x_rows, qkv_to = together(x_rows, qkv_to)
    unit_one, inv_one = norm_parts(x_rows)
    unit_low, cond_low = together(unit_one.astype(BF16), cond_low)
    unit_all = lax.all_gather(unit_low, "narrow", axis=0, tiled=True)
    mod_part = dot(cond_low, w_ada)[0] + b_ada.astype(F32)
    small = jnp.concatenate([mod_part] + [v.astype(F32) for v in (qv_bias, b_out, b_fc1, b_fc2)])
    small_all = ring_gather(small)
    ends = [0]
    for piece in (mod_part, qv_bias, b_out, b_fc1, b_fc2):
        ends.append(ends[-1] + piece.shape[0])
    modulation, qv_full, bout_full, bfc1_full, bfc2_full = [
        small_all[:, low:high].reshape(-1) for low, high in zip(ends[:-1], ends[1:])
    ]
    shift_one, scale_one, gate_one, shift_two, scale_two, gate_two = [
        modulation[None, k * width : (k + 1) * width] for k in range(6)
    ]

    qkv_cols = quad_gather(exchange(qkv_to, "narrow"))
    qkv_cols = qkv_cols.transpose(1, 0, 2, 3).reshape(width, 3 * cols)

    (pack,) = call(
        functools.partial(pack_kernel, n, w),
        (jnp.asarray(p, jnp.int32).reshape(1), w_fc1, w_fc2),
        [((2 * hidden_dev, width), BF16)],
        scalars=1,
        name="pack",
        micros=3,
    )

    out_mine = lax.dynamic_slice_in_dim(w_out, quad_index(0) * sub, sub, 0)
    grad_out = living * d_out.reshape(tokens, width)
    grad_two = (gate_two * grad_out).astype(BF16)
    two_own = share(grad_two, "chip")
    unit_all, out_mine, pack = together(unit_all, out_mine, pack)
    out_ring = [out_mine] + [ring(out_mine, j) for j in range(1, n)]

    pack_all = lax.all_gather(pack, "narrow", axis=0, tiled=False)
    bfc1_dev = lax.dynamic_index_in_dim(bfc1_full.reshape(n, w, hidden_dev), p, 1, keepdims=False)
    bfc1_dev = bfc1_dev.reshape(1, hidden_all)

    qv_two = qv_full.reshape(2, n, cols)
    q_bias = lax.dynamic_index_in_dim(qv_two[0], z, 0, keepdims=True)
    v_bias = lax.dynamic_index_in_dim(qv_two[1], z, 0, keepdims=True)
    bias_three = jnp.concatenate([q_bias, jnp.zeros_like(q_bias), v_bias], axis=1)
    wide_cols = 3 * heads * LANES
    mod_one = jnp.concatenate([shift_one, scale_one], axis=0)
    mixed, projected, lse, qkv_wide = call(
        functools.partial(attend_kernel, n, heads, score_scale),
        (unit_all, mod_one, qkv_cols, bias_three),
        [
            ((n, tokens, cols), BF16),
            ((image, wide_cols), BF16),
            ((8, image), F32),
            ((width, wide_cols), BF16),
        ],
        name="attend",
        micros=26,
    )
    mixed, two_own, *out_ring = together(mixed, two_own, *out_ring)
    two_other = flip(two_own, "core", 1)
    mixed_heads = mixed
    out_quad = quad_gather(place(out_ring, lambda j: lax.rem(z + n - j, n)))
    out_all = out_quad.transpose(1, 0, 2, 3).reshape(width, width)
    mixed = exchange(mixed, "narrow")
    mixed, out_all, pack_all = together(mixed, out_all, pack_all)
    mixed_cat = mixed.transpose(1, 0, 2).reshape(tokens, width)

    branch_one = dot(mixed_cat, out_all) + bout_full[None]
    middle = x_rows + gate_one * branch_one
    unit_two, inv_two = norm_parts(middle)
    second_low = (unit_two * (1.0 + scale_two) + shift_two).astype(BF16)

    core_at = jnp.asarray(lax.axis_index("core"), jnp.int32).reshape(1)
    second_own, second_other = plane_share(second_low)
    side = ((chips, tokens, width), BF16)
    second_terms_own, second_terms_other, two_terms_own, two_terms_other, fc_terms, bfc1_terms = call(
        functools.partial(mlp_kernel, n),
        (second_own, second_other, two_own, two_other, pack_all, bfc1_dev),
        [side, side, side, side, ((n, 2 * hidden_dev, width), BF16), ((8, hidden_all), F32)],
        [
            ((width, hidden_all), BF16),
            ((hidden_all, width), BF16),
            ((w * tokens, hidden_all), BF16),
            ((w * tokens, hidden_all), BF16),
            ((width, hidden_all), F32),
        ],
        name="mlp",
        micros=33,
    )
    bfc1_terms = bfc1_terms[0]
    fc_own = lax.psum_scatter(fc_terms, "narrow", scatter_dimension=0, tiled=False)
    grad_second = add_up(exchange(core_add(second_terms_own, second_terms_other), "chip"))
    two_terms = core_add(two_terms_own, two_terms_other)
    grad_second, two_terms = together(grad_second, two_terms)

    bfc2_terms = jnp.sum(grad_two.astype(F32), axis=0)

    grad_shift_two = jnp.sum(grad_second, axis=0)
    grad_scale_two = jnp.sum(grad_second * unit_two, axis=0)
    grad_middle = grad_out + norm_back(unit_two, inv_two, grad_second * (1.0 + scale_two))
    grad_one = (gate_one * grad_middle).astype(BF16)
    grad_gate_one = jnp.sum(grad_middle * branch_one, axis=0)
    bout_terms = jnp.sum(grad_one.astype(F32), axis=0)
    grad_mixed_cat = dot(grad_one, out_all, ((1,), (1,))).astype(BF16).reshape(tokens, n, cols)
    grad_mixed_cat, fc_own, mixed_cat, grad_one = together(
        grad_mixed_cat, fc_own, mixed_cat, grad_one
    )
    fc_all = lax.all_gather(fc_own, plane, axis=0, tiled=False)
    branch_two = chip_sum(two_terms)
    grad_mixed = exchange(grad_mixed_cat.transpose(1, 0, 2), "narrow")
    branch_two = branch_two + bfc2_full[None]
    result = living * (middle + gate_two * branch_two)
    grad_gate_two = jnp.sum(grad_out * branch_two, axis=0)
    piece = shard // w
    padded = -(-piece // 8) * 8
    wout_sides = call(
        functools.partial(wout_kernel, n),
        (core_at, mixed_cat, grad_one),
        [((chips, n, padded, width), BF16)] * 2,
        [((width, width), F32), ((2, chips, n, padded, width), BF16)],
        name="wout_terms",
        scalars=1,
        micros=4,
    )
    wout_low = core_add(*wout_sides)
    grad_mixed, wout_low = together(grad_mixed, wout_low)
    wout_sum = add_up(exchange(wout_low, "chip")).astype(BF16)

    wqkv_side = ((chips, n, padded, 3 * cols), BF16)
    wqkv_own, wqkv_other, grad_projected, projected_sums = call(
        functools.partial(attend_back_kernel, n, heads, score_scale),
        (core_at, projected, lse, grad_mixed, mixed_heads, unit_all, mod_one),
        [wqkv_side, wqkv_side, ((image, wide_cols), BF16), ((8, wide_cols), F32)],
        [
            ((image, heads * LANES), BF16),
            ((8, image), F32),
            ((image, width), BF16),
            ((width, 3 * cols), F32),
            ((LANES, image), F32),
            ((2, chips, n, padded, 3 * cols), BF16),
        ],
        name="attend_back",
        scalars=1,
        micros=28,
    )
    first_terms, one_sums = call(
        functools.partial(first_kernel, n),
        (grad_projected, qkv_wide, unit_all),
        [((n, tokens, width), BF16), ((8, width), F32)],
        name="first_terms",
        micros=10,
    )
    grad_shift_one = one_sums[0]
    grad_scale_one = one_sums[1]
    grad_first = lax.psum_scatter(first_terms, "narrow", scatter_dimension=0, tiled=False)
    grad_first = grad_first.astype(F32)
    grad_input = grad_middle + norm_back(unit_one, inv_one, grad_first * (1.0 + scale_one))

    projected_sums = projected_sums[0].reshape(3, heads, LANES)[:, :, :head_size].reshape(3, cols)

    mod_terms = jnp.concatenate(
        [grad_shift_one, grad_scale_one, grad_gate_one, grad_shift_two, grad_scale_two, grad_gate_two]
    ).reshape(n, -1)
    qv_terms = jnp.zeros((2, n, cols), F32)
    qv_terms = lax.dynamic_update_slice(
        qv_terms, jnp.stack([projected_sums[0], projected_sums[2]])[:, None], (0, z, 0)
    )
    bfc1_wide = lax.dynamic_update_slice(
        jnp.zeros((n, w, hidden_dev), F32), bfc1_terms.reshape(n, 1, hidden_dev), (0, p, 0)
    )
    small_terms = jnp.concatenate(
        [
            mod_terms,
            qv_terms.reshape(n, -1),
            bout_terms.reshape(n, -1),
            bfc1_wide.reshape(n, -1),
            bfc2_terms.reshape(n, -1),
        ],
        axis=1,
    )
    wqkv_low = core_add(wqkv_own, wqkv_other)
    wqkv_sum = add_up(exchange(wqkv_low, "chip")).astype(BF16)
    wqkv_sum, small_terms, wout_sum = together(wqkv_sum, small_terms, wout_sum)
    wqkv_got = exchange(jnp.concatenate([wqkv_sum, wout_sum], axis=2), "narrow")
    wout_own = add_up(wqkv_got[:, :, 3 * cols :]).astype(BF16)
    wqkv_got, fc_all = together(wqkv_got[:, :, : 3 * cols], fc_all)
    small_own = ring_sum(small_terms)
    mod_size = mod_terms.shape[1]
    mod_low = small_own[:mod_size].astype(BF16)
    cond_part = dot(mod_low[None], w_ada, ((1,), (1,)))
    cond_total = jnp.sum(ring_gather(cond_part), axis=0)
    shared = plane_rows(jnp.concatenate([small_own, cond_act[0]]))
    grad_wfc1, grad_wfc2 = call(
        functools.partial(unpack_kernel, n),
        (fc_all,),
        [((shard, n * w * hidden_dev), F32), ((w * hidden_dev, width), F32)],
        name="unpack",
        micros=8,
    )
    wqkv_mine, wqkv_theirs = plane_share(wqkv_got)
    wout_mine, wout_theirs = plane_share(wout_own)
    grad_wout = place([wout_mine, wout_theirs], lambda r: lax.axis_index("core") ^ r)
    grad_wout = grad_wout.transpose(1, 0, 2, 3)[:, :, :piece].reshape(shard, width).astype(F32)
    (grad_wqkv,) = call(
        functools.partial(unpack_qkv_kernel, n),
        (core_at, wqkv_mine, wqkv_theirs),
        [((shard, 3 * width), F32)],
        scalars=1,
        name="unpack_qkv",
        micros=4,
    )
    grad_condition = silu_pull(cond_total)[0]
    mod_rows = shared[:, :mod_size].astype(BF16)
    cond_rows = shared[:, small_own.shape[0] :].astype(BF16)
    grad_wada = dot(cond_rows, mod_rows, ((0,), (0,)))
    grad_bada = jnp.sum(mod_rows.astype(F32), axis=0)
    bias_sums = jnp.sum(shared[:, mod_size : small_own.shape[0]], axis=0)
    ends = [0]
    for piece in (qv_bias, b_out, b_fc1, b_fc2):
        ends.append(ends[-1] + piece.shape[0])
    grad_qv, grad_bout, grad_bfc1, grad_bfc2 = [
        bias_sums[low:high] for low, high in zip(ends[:-1], ends[1:])
    ]
    return (
        result[None],
        grad_input[None],
        grad_condition,
        grad_wada,
        grad_bada,
        grad_wqkv,
        grad_qv,
        grad_wout,
        grad_bout,
        grad_wfc1,
        grad_bfc1,
        grad_wfc2,
        grad_bfc2,
    )


def solution(mesh):
    narrow = mesh.shape["narrow"]
    mesh = Mesh(mesh.devices.reshape(-1, 2, narrow), ("chip", "core", "narrow"))
    in_specs = (
        P(WIDE, "narrow", None),
        P(WIDE, None),
        P(WIDE),
        P(None, "narrow"),
        P("narrow"),
        P("narrow", None),
        P("narrow"),
        P("narrow", None),
        P("narrow"),
        P("narrow", None),
        P("narrow"),
        P("narrow", None),
        P("narrow"),
        P(WIDE, "narrow", None),
    )
    out_specs = (
        P(WIDE, "narrow", None),
        P(WIDE, "narrow", None),
        P(WIDE, None),
        P(None, "narrow"),
        P("narrow"),
        P("narrow", None),
        P("narrow"),
        P("narrow", None),
        P("narrow"),
        P("narrow", None),
        P("narrow"),
        P("narrow", None),
        P("narrow"),
    )
    return jax.shard_map(
        per_device, mesh=mesh, in_specs=in_specs, out_specs=out_specs, check_vma=False
    )
```

```python
import functools
import math

import jax
import jax.numpy as jnp
from jax import lax
from jax.experimental import pallas as pl
from jax.experimental.pallas import tpu as pltpu
from jax.sharding import Mesh
from jax.sharding import PartitionSpec as P

HEADS = 16
WIDE = ("chip", "core")
F32 = jnp.float32
BF16 = jnp.bfloat16
LANES = 128
ROOT = math.sqrt(2 / math.pi)


def dot(left, right, dims=((1,), (0,))):
    return lax.dot_general(left, right, (dims, ((), ())), preferred_element_type=F32)


def flip(block, axis, bit):
    size = lax.axis_size(axis)
    return lax.ppermute(block, axis, [(i, i ^ bit) for i in range(size)])


def exchange(blocks, axis):
    return lax.all_to_all(blocks, axis, 0, 0, tiled=False)


def share(block, axis):
    return exchange(jnp.broadcast_to(block[None], (lax.axis_size(axis),) + block.shape), axis)


def ring(block, step):
    n = lax.axis_size("narrow")
    return lax.ppermute(block, "narrow", [(i, (i + step) % n) for i in range(n)])


def pick(blocks, index):
    return lax.dynamic_index_in_dim(blocks, index, 0, keepdims=False)


def together(*values):
    return lax.optimization_barrier(values)


def add_up(blocks):
    return sum(blocks[i].astype(F32) for i in range(blocks.shape[0]))


def place(blocks, index_of):
    buffer = jnp.zeros((len(blocks),) + blocks[0].shape, blocks[0].dtype)
    for j, block in enumerate(blocks):
        buffer = lax.dynamic_update_index_in_dim(buffer, block, index_of(j), 0)
    return buffer


def quad_index(r):
    chip = lax.axis_index("chip")
    core = lax.axis_index("core")
    return 2 * ((chip & 1) ^ (r >> 1)) + (core ^ (r & 1))


def quad_gather(block):
    two = flip(block, "chip", 1)
    pair = flip(jnp.stack([block, two]), "core", 1)
    return place([block, pair[0], two, pair[1]], quad_index)


def ring_gather(block):
    n = lax.axis_size("narrow")
    z = lax.axis_index("narrow")
    blocks = [block] + [ring(block, j) for j in range(1, n)]
    return place(blocks, lambda j: lax.rem(z + n - j, n))


def as_rows(values, columns):
    high = values.astype(BF16)
    low = (values - high.astype(F32)).astype(BF16)
    both = jnp.concatenate([high, low], axis=1)
    rows = -(-both.shape[1] // (8 * columns)) * 8
    both = jnp.pad(both, ((0, 0), (0, rows * columns - both.shape[1])))
    return both.reshape(-1, rows, columns)


def from_rows(rows, size):
    both = rows.reshape(rows.shape[0], -1).astype(F32)
    return both[:, :size] + both[:, size : 2 * size]


def plane_share(block):
    own = share(block, "chip")
    return own, flip(own, "core", 1)


def core_add(own, other):
    return (own.astype(F32) + flip(other, "core", 1).astype(F32)).astype(BF16)


def call(kernel, args, outs, scratch=(), scalars=0, name=None, micros=1, space=pltpu.VMEM):
    vmem = pl.BlockSpec(memory_space=pltpu.VMEM)
    given = pl.BlockSpec(memory_space=space)
    smem = pl.BlockSpec(memory_space=pltpu.SMEM)
    return pl.pallas_call(
        kernel,
        out_shape=tuple(jax.ShapeDtypeStruct(shape, dtype) for shape, dtype in outs),
        in_specs=[smem if i < scalars else given for i in range(len(args))],
        out_specs=tuple(vmem for _ in outs),
        scratch_shapes=[
            part if isinstance(part, pltpu.SemaphoreType) else pltpu.VMEM(*part) for part in scratch
        ],
        compiler_params=pltpu.CompilerParams(vmem_limit_bytes=56 << 20),
        cost_estimate=pl.CostEstimate(
            flops=1000000000 * micros, bytes_accessed=3000000 * micros, transcendentals=0
        ),
        name=name,
    )(*args)


def pack_kernel(n, w, p_ref, fc1_ref, fc2_ref, first_ref, second_ref):
    shard = fc1_ref.shape[0]
    rows = fc2_ref.shape[0] // w
    full = fc2_ref.shape[0]
    for q in range(w):

        @pl.when(p_ref[0] == q)
        def _(q=q):
            second_ref[...] = fc2_ref[q * rows : (q + 1) * rows]
            pieces = [
                fc1_ref[part : part + rows, a * full + q * rows : a * full + (q + 1) * rows]
                for part in range(0, shard, rows)
                for a in range(n)
            ]
            first_ref[...] = jnp.concatenate(pieces, axis=1)


def qkv_kernel(n, place_ref, w_ref, out_ref):
    sub = out_ref.shape[1]
    cols = out_ref.shape[2] // 3
    width = w_ref.shape[1] // 3
    for q in range(w_ref.shape[0] // sub):

        @pl.when(place_ref[0] == q)
        def _(q=q):
            for a in range(n):
                out_ref[a] = jnp.concatenate(
                    [
                        w_ref[q * sub : (q + 1) * sub, t * width + a * cols : t * width + (a + 1) * cols]
                        for t in range(3)
                    ],
                    axis=1,
                )


def attend_kernel(
    n, heads, scale, unit_ref, mod_ref, w_ref, bias_ref, mixed_ref, proj_ref, lse_ref, wide_ref
):
    width = unit_ref.shape[2]
    image = proj_ref.shape[0]
    tokens = image // n
    cols = w_ref.shape[1] // 3
    size = cols // heads
    pad = jnp.zeros((width, LANES - size), BF16)
    pad_row = jnp.zeros((1, LANES - size), F32)
    bias = []
    for t in range(3 * heads):
        wide_ref[:, t * LANES : (t + 1) * LANES] = jnp.concatenate(
            [w_ref[:, t * size : (t + 1) * size], pad], axis=1
        )
        bias += [bias_ref[:, t * size : (t + 1) * size], pad_row]
    bias = jnp.concatenate(bias, axis=1)
    gain = 1.0 + mod_ref[1:2]
    shift = mod_ref[0:1]

    def project(i, carry):
        rows = pl.ds(pl.multiple_of(i * tokens, tokens), tokens)
        first = (unit_ref[i, :tokens].astype(F32) * gain + shift).astype(BF16)
        proj_ref[rows] = (dot(first, wide_ref[...]) + bias).astype(BF16)
        return carry

    lax.fori_loop(0, n, project, 0)
    for h in range(heads):
        keys = proj_ref[:, (heads + h) * LANES : (heads + h + 1) * LANES]
        values = proj_ref[:, (2 * heads + h) * LANES : (2 * heads + h + 1) * LANES]
        values_t = values.T

        def block(i, carry, h=h, keys=keys, values_t=values_t):
            rows = pl.ds(pl.multiple_of(i * tokens, tokens), tokens)
            queries = proj_ref[rows, h * LANES : (h + 1) * LANES]
            scores = dot(keys, queries, ((1,), (1,)))
            top = jnp.max(scores, axis=0, keepdims=True)
            grown = jnp.exp((scores - top) * scale)
            total = jnp.sum(grown, axis=0, keepdims=True)
            mixed = dot(values_t, grown.astype(BF16)) / total
            mixed = mixed.T[:, :size].astype(BF16)
            for q in range(n):
                at = q * cols + h * size
                mixed_ref[i, :, at : at + size] = mixed[q * tokens // n : (q + 1) * tokens // n]
            lse_ref[h : h + 1, rows] = top * scale + jnp.log(total)
            return carry

        lax.fori_loop(0, n, block, 0)


def attend_back_kernel(
    n,
    heads,
    scale,
    core_ref,
    proj_ref,
    lse_ref,
    grad_ref,
    mixed_ref,
    unit_ref,
    mod_ref,
    wide_ref,
    *rest,
):
    terms_own_ref, terms_other_ref, first_ref, last_ref, sums_ref, proj_sums_ref = rest[:6]
    grad_proj, grad_wide, delta_ref, first_low, terms, query_acc, terms_low = rest[6:]
    width = unit_ref.shape[2]
    image = proj_ref.shape[0]
    tokens = image // n
    cols = grad_ref.shape[2] // n
    size = cols // heads
    pad = jnp.zeros((tokens, LANES - size), BF16)
    ones = jnp.ones((8, LANES), F32)
    gain = 1.0 + mod_ref[1:2]
    shift = mod_ref[0:1]

    def prepare(i, carry):
        rows = pl.ds(pl.multiple_of(i * tokens, tokens), tokens)
        for h in range(heads):
            lanes = [slice(q * cols + h * size, q * cols + (h + 1) * size) for q in range(n)]
            grad = jnp.concatenate([grad_ref[i, :, at] for at in lanes], axis=0)
            mixed = jnp.concatenate([mixed_ref[i, :, at] for at in lanes], axis=0)
            grad = jnp.concatenate([grad, pad], axis=1)
            mixed = jnp.concatenate([mixed, pad], axis=1)
            grad_wide[rows, h * LANES : (h + 1) * LANES] = grad
            both = grad.astype(F32) * mixed.astype(F32)
            delta = lax.dot_general(
                ones, both, (((1,), (1,)), ((), ())),
                preferred_element_type=F32, precision=lax.Precision.HIGHEST,
            )
            delta_ref[h : h + 1, rows] = delta[0:1]
        first_low[rows] = (unit_ref[i, :tokens].astype(F32) * gain + shift).astype(BF16)
        return carry

    lax.fori_loop(0, n, prepare, 0)
    for h in range(heads):
        q_at = slice(h * LANES, (h + 1) * LANES)
        k_at = slice((heads + h) * LANES, (heads + h + 1) * LANES)
        v_at = slice((2 * heads + h) * LANES, (2 * heads + h + 1) * LANES)
        query_acc[...] = jnp.zeros_like(query_acc)

        def block(j, carry, h=h, q_at=q_at, k_at=k_at, v_at=v_at):
            rows = pl.ds(pl.multiple_of(j * tokens, tokens), tokens)
            keys = proj_ref[rows, k_at]
            values = proj_ref[rows, v_at]
            queries = proj_ref[:, q_at]
            grads = grad_wide[:, q_at]
            weights = jnp.exp(dot(keys, queries, ((1,), (1,))) * scale - lse_ref[h : h + 1])
            grad_weights = dot(values, grads, ((1,), (1,)))
            grad_scores = (weights * (grad_weights - delta_ref[h : h + 1])).astype(BF16)
            grad_proj[rows, v_at] = dot(weights.astype(BF16), grads).astype(BF16)
            grad_proj[rows, k_at] = (dot(grad_scores, queries) * scale).astype(BF16)
            query_acc[...] += dot(keys.T, grad_scores)
            return carry

        lax.fori_loop(0, n, block, 0)
        grad_proj[:, q_at] = (query_acc[...] * scale).T.astype(BF16)

    proj_sums_ref[...] = jnp.zeros_like(proj_sums_ref)
    sums_ref[...] = jnp.zeros_like(sums_ref)

    def out(i, carry):
        rows = pl.ds(pl.multiple_of(i * tokens, tokens), tokens)
        block = grad_proj[rows]
        grad = dot(block, wide_ref[...], ((1,), (1,)))
        proj_sums_ref[0:1] += jnp.sum(block.astype(F32), axis=0, keepdims=True)
        sums_ref[0:1] += jnp.sum(grad, axis=0, keepdims=True)
        sums_ref[1:2] += jnp.sum(grad * unit_ref[i, :tokens].astype(F32), axis=0, keepdims=True)
        first_ref[i] = grad[: tokens // 2].astype(BF16)
        last_ref[i] = grad[tokens // 2 :].astype(BF16)
        return carry

    lax.fori_loop(0, n, out, 0)
    for t in range(3):
        part = dot(
            first_low[...], grad_proj[:, t * heads * LANES : (t + 1) * heads * LANES], ((0,), (0,))
        )
        terms[:, t * cols : (t + 1) * cols] = jnp.concatenate(
            [part[:, h * LANES : h * LANES + size] for h in range(heads)], axis=1
        )
    if terms.shape[1] > 3 * cols:
        terms[:, 3 * cols :] = jnp.zeros((width, terms.shape[1] - 3 * cols), F32)

    def store(q, a, block):
        terms_low[q % 2, q // 2, a] = block

    to_pieces(terms, store, n, 2 * terms_own_ref.shape[0], terms_own_ref.shape[2])
    terms_own_ref[...] = terms_low[core_ref[0]]
    terms_other_ref[...] = terms_low[1 - core_ref[0]]


def to_pieces(terms, store, n, w, padded):
    columns = terms.shape[1]
    shard = terms.shape[0] // n
    piece = shard // w
    for a in range(n):
        for q in range(w):
            at = a * shard + q * piece
            block = terms[at : at + piece].astype(BF16)
            if padded > piece:
                block = jnp.concatenate([block, jnp.zeros((padded - piece, columns), BF16)], axis=0)
            store(q, a, block)


def wout_kernel(n, core_ref, mixed_ref, grad_ref, own_ref, other_ref, terms, low):
    step = grad_ref.shape[1] // 3
    for t in range(3):
        lanes = slice(t * step, (t + 1) * step)
        terms[:, lanes] = dot(mixed_ref[...], grad_ref[:, lanes], ((0,), (0,)))
    _, chips, _, padded, _ = low.shape

    def store(q, a, block):
        low[q % 2, q // 2, a] = block

    to_pieces(terms, store, n, 2 * chips, padded)
    for a in range(n):
        own_ref[:, a * padded : (a + 1) * padded] = low[core_ref[0], :, a]
        other_ref[:, a * padded : (a + 1) * padded] = low[1 - core_ref[0], :, a]


def middle_kernel(
    n, quad_ref, got_ref, x_ref, mod_ref, bias_ref, *rest
):
    part_refs, (mixed_ref, out_ref, branch_ref, middle_ref, second_ref) = rest[:4], rest[4:]
    rows = got_ref.shape[1]
    cols = got_ref.shape[2] // n
    sub = part_refs[0].shape[1]
    for place_at in range(4):

        @pl.when(quad_ref[0] == place_at)
        def _(place_at=place_at):
            for r in range(4):
                for a in range(n):
                    at = (4 * a + (place_at ^ r)) * sub
                    out_ref[at : at + sub] = part_refs[r][a]

    for q in range(n):
        mixed_ref[q * rows : (q + 1) * rows] = jnp.concatenate(
            [got_ref[j, :, q * cols : (q + 1) * cols] for j in range(n)], axis=1
        )
    branch = dot(mixed_ref[...], out_ref[...]) + bias_ref[...]
    middle = x_ref[...] + mod_ref[2:3] * branch
    unit, _ = norm_parts(middle)
    branch_ref[...] = branch
    middle_ref[...] = middle
    second = (unit * (1.0 + mod_ref[4:5]) + mod_ref[3:4]).astype(BF16)
    for k in range(second_ref.shape[0]):
        second_ref[k] = second


def middle_back_kernel(
    n, came_ref, middle_ref, branch_ref, d_out_ref, mod_ref, out_ref, *rest
):
    grad_middle_ref, grad_one_ref, mixed_ref, sums_ref = rest
    rows = mixed_ref.shape[1]
    cols = mixed_ref.shape[2] // n
    unit, inv = norm_parts(middle_ref[...])
    grad_second = came_ref[0].astype(F32)
    for r in range(1, came_ref.shape[0]):
        grad_second += came_ref[r].astype(F32)
    grad_middle = d_out_ref[...] + norm_back(unit, inv, grad_second * (1.0 + mod_ref[4:5]))
    grad_one = (mod_ref[2:3] * grad_middle).astype(BF16)
    grad_middle_ref[...] = grad_middle
    grad_one_ref[...] = grad_one
    parts = (grad_second, grad_second * unit, grad_middle * branch_ref[...], grad_one.astype(F32))
    for k, part in enumerate(parts):
        sums_ref[k : k + 1] = jnp.sum(part, axis=0, keepdims=True)
    mixed = dot(grad_one, out_ref[...], ((1,), (1,))).astype(BF16)
    for j in range(n):
        mixed_ref[j] = jnp.concatenate(
            [mixed[q * rows : (q + 1) * rows, j * cols : (j + 1) * cols] for q in range(n)], axis=1
        )


def mlp_kernel(
    n,
    own_ref,
    other_ref,
    two_own_ref,
    two_other_ref,
    pack_one_ref,
    pack_two_ref,
    bias_ref,
    second_own_ref,
    second_other_ref,
    two_sum_own_ref,
    two_sum_other_ref,
    grad_ref,
    bias_grad_ref,
    fc1,
    fc2,
    active_all,
    hidden_all,
    grad_fc1,
):
    chips, tokens, width = own_ref.shape
    rows = pack_one_ref.shape[1]
    units = n * rows
    halves = width // units
    for a in range(n):
        fc2[a * rows : (a + 1) * rows] = pack_two_ref[a]
        for part in range(halves):
            at = (a * halves + part) * rows
            fc1[at : at + rows] = pack_one_ref[a, :, part * units : (part + 1) * units]
    bias_grad_ref[...] = jnp.zeros_like(bias_grad_ref)
    sides = (
        (own_ref, two_own_ref, second_own_ref, two_sum_own_ref),
        (other_ref, two_other_ref, second_other_ref, two_sum_other_ref),
    )
    for side, refs in enumerate(sides):

        def block(i, carry, side=side, refs=refs):
            x_ref, g_ref, second_ref, two_ref = refs
            at = pl.ds(pl.multiple_of((side * chips + i) * tokens, tokens), tokens)
            hidden = dot(x_ref[i], fc1[...]) + bias_ref[...]
            square = hidden * hidden
            inner = ROOT * (hidden + 0.044715 * square * hidden)
            bend = jnp.tanh(inner)
            half = 0.5 * (1.0 + bend)
            active = (hidden * half).astype(BF16)
            slope = half + 0.5 * hidden * (1.0 - bend * bend) * (ROOT * (1.0 + 3 * 0.044715 * square))
            grad = (dot(g_ref[i], fc2[...], ((1,), (1,))) * slope).astype(BF16)
            active_all[at] = active
            hidden_all[at] = grad
            second_ref[i] = dot(grad, fc1[...], ((1,), (1,))).astype(BF16)
            two_ref[i] = dot(active, fc2[...]).astype(BF16)
            bias_grad_ref[0:1] += jnp.sum(grad.astype(F32), axis=0, keepdims=True)
            return carry

        lax.fori_loop(0, chips, block, 0)
    step = width // 3
    half_rows = chips * tokens
    for t in range(3):
        lanes = slice(t * step, (t + 1) * step)
        part = dot(
            active_all[:half_rows], two_own_ref[:, :, lanes].reshape(half_rows, step), ((0,), (0,))
        ) + dot(
            active_all[half_rows:], two_other_ref[:, :, lanes].reshape(half_rows, step), ((0,), (0,))
        )
        for a in range(n):
            grad_ref[a, :rows, lanes] = part[a * rows : (a + 1) * rows].astype(BF16)
        grad_fc1[lanes] = dot(
            own_ref[:, :, lanes].reshape(half_rows, step), hidden_all[:half_rows], ((0,), (0,))
        ) + dot(
            other_ref[:, :, lanes].reshape(half_rows, step), hidden_all[half_rows:], ((0,), (0,))
        )
    for a in range(n):
        grad_ref[a, rows:] = jnp.concatenate(
            [
                grad_fc1[(a * halves + part) * rows : (a * halves + part + 1) * rows].astype(BF16)
                for part in range(halves)
            ],
            axis=1,
        )


def unpack_kernel(n, got_ref, fc1_ref, fc2_ref):
    w, _, width = got_ref.shape
    rows = got_ref.shape[1] // 2
    units = n * rows
    full = w * rows
    for q in range(w):
        fc2_ref[q * rows : (q + 1) * rows] = got_ref[q, :rows].astype(F32)
    for part in range(width // units):
        for a in range(n):
            at = part * units + a * rows
            fc1_ref[part * rows : (part + 1) * rows, a * full : (a + 1) * full] = jnp.concatenate(
                [got_ref[q, rows:, at : at + rows].astype(F32) for q in range(w)], axis=1
            )


def unpack_qkv_kernel(
    n, padded, cols, core_ref, own_from, other_from, out_ref, wout_ref, own_ref, other_ref, own_sem, other_sem
):
    chips = own_ref.shape[0]
    piece = out_ref.shape[0] // (2 * chips)
    own_copy = pltpu.make_async_copy(own_from, own_ref, own_sem)
    other_copy = pltpu.make_async_copy(other_from, other_ref, other_sem)
    own_copy.start()
    other_copy.start()
    own_copy.wait()
    other_copy.wait()
    parts = -(-wout_ref.shape[1] // own_ref.shape[2])
    part = wout_ref.shape[1] // parts
    for core in range(2):

        @pl.when(core_ref[0] == core)
        def _(core=core):
            for q in range(2 * chips):
                got_ref = own_ref if q % 2 == core else other_ref
                out_ref[q * piece : (q + 1) * piece] = jnp.concatenate(
                    [
                        got_ref[q // 2, a * padded : a * padded + piece, t * cols : (t + 1) * cols]
                        .astype(F32)
                        for t in range(3)
                        for a in range(n)
                    ],
                    axis=1,
                )
                wout_ref[q * piece : (q + 1) * piece] = jnp.concatenate(
                    [
                        got_ref[q // 2, a * padded : a * padded + piece, :part].astype(F32)
                        for a in range(n, n + parts)
                    ],
                    axis=1,
                )


def rows_mean(rows_in):
    return jnp.mean(rows_in, axis=-1, keepdims=True)


def norm_parts(rows_in):
    centered = rows_in - rows_mean(rows_in)
    inv = lax.rsqrt(rows_mean(centered * centered) + 1e-06)
    return centered * inv, inv


def norm_back(unit, inv, grad_unit):
    return inv * (grad_unit - rows_mean(grad_unit) - unit * rows_mean(grad_unit * unit))


def per_device(
    x_input,
    condition,
    counts,
    w_ada,
    b_ada,
    w_qkv,
    qv_bias,
    w_out,
    b_out,
    w_fc1,
    b_fc1,
    w_fc2,
    b_fc2,
    d_out,
):
    n = lax.axis_size("narrow")
    chips = lax.axis_size("chip")
    w = 2 * chips
    z = lax.axis_index("narrow")
    p = 2 * lax.axis_index("chip") + lax.axis_index("core")
    plane = ("chip", "core")
    slot_count, tokens, width = x_input.shape
    x_rows = x_input.reshape(tokens, width)
    heads = HEADS // n
    head_size = width // HEADS
    score_scale = head_size ** (-0.5)
    shard = width // n
    sub = shard // 4
    hidden_dev = w_fc2.shape[0] // w
    hidden_all = n * hidden_dev
    cols = heads * head_size
    image = n * tokens

    living = (counts[0] > 0).astype(F32)

    quad_at = jnp.asarray(quad_index(0), jnp.int32).reshape(1)
    (qkv_to,) = call(
        functools.partial(qkv_kernel, n),
        (quad_at, w_qkv),
        [((n, sub, 3 * cols), BF16)],
        scalars=1,
        name="qkv_to",
        micros=3,
    )

    qkv_cols = quad_gather(exchange(qkv_to, "narrow"))
    qkv_cols = qkv_cols.transpose(1, 0, 2, 3).reshape(width, 3 * cols)

    cond_act, silu_pull = jax.vjp(jax.nn.silu, condition)
    cond_low = cond_act.astype(BF16)
    x_rows, qkv_to = together(x_rows, qkv_to)
    unit_one, inv_one = norm_parts(x_rows)
    unit_low, cond_low = together(unit_one.astype(BF16), cond_low)
    out_mine = lax.dynamic_slice_in_dim(w_out, quad_index(0) * sub, sub, 0)
    unit_all = lax.all_gather(
        jnp.concatenate([unit_low, out_mine]), "narrow", axis=0, tiled=False
    )
    mod_part = dot(cond_low, w_ada)[0] + b_ada.astype(F32)
    small = jnp.concatenate([mod_part] + [v.astype(F32) for v in (qv_bias, b_out, b_fc1, b_fc2)])
    small_all = ring_gather(small)
    ends = [0]
    for piece in (mod_part, qv_bias, b_out, b_fc1, b_fc2):
        ends.append(ends[-1] + piece.shape[0])
    modulation, qv_full, bout_full, bfc1_full, bfc2_full = [
        small_all[:, low:high].reshape(-1) for low, high in zip(ends[:-1], ends[1:])
    ]
    shift_one, scale_one, gate_one, shift_two, scale_two, gate_two = [
        modulation[None, k * width : (k + 1) * width] for k in range(6)
    ]


    pack_one, pack_two = call(
        functools.partial(pack_kernel, n, w),
        (jnp.asarray(p, jnp.int32).reshape(1), w_fc1, w_fc2),
        [((hidden_dev, width), BF16)] * 2,
        scalars=1,
        name="pack",
        micros=3,
    )

    core = lax.axis_index("core")
    grad_out = living * d_out.reshape(tokens, width)
    grad_two = (gate_two * grad_out).astype(BF16)
    two_own = share(grad_two, "chip")
    unit_all, pack_one = together(unit_all, pack_one)
    out_quad = unit_all[:, tokens:]
    out_two = flip(out_quad, "chip", 1)
    pack_one = lax.all_gather(pack_one, "narrow", axis=0, tiled=False)
    bfc1_dev = lax.dynamic_index_in_dim(bfc1_full.reshape(n, w, hidden_dev), p, 1, keepdims=False)
    bfc1_dev = bfc1_dev.reshape(1, hidden_all)

    qv_two = qv_full.reshape(2, n, cols)
    q_bias = lax.dynamic_index_in_dim(qv_two[0], z, 0, keepdims=True)
    v_bias = lax.dynamic_index_in_dim(qv_two[1], z, 0, keepdims=True)
    bias_three = jnp.concatenate([q_bias, jnp.zeros_like(q_bias), v_bias], axis=1)
    wide_cols = 3 * heads * LANES
    mod_one = jnp.concatenate([shift_one, scale_one], axis=0)
    mixed, projected, lse, qkv_wide = call(
        functools.partial(attend_kernel, n, heads, score_scale),
        (unit_all, mod_one, qkv_cols, bias_three),
        [
            ((n, tokens // n, width), BF16),
            ((image, wide_cols), BF16),
            ((8, image), F32),
            ((width, wide_cols), BF16),
        ],
        name="attend",
        micros=26,
    )
    mixed, two_own, out_two = together(mixed, two_own, out_two)
    two_other = flip(two_own, "core", 1)
    mixed_heads = mixed
    out_pair = flip(jnp.stack([out_quad, out_two]), "core", 1)
    mixed = exchange(mixed, "narrow")
    mixed, out_pair, pack_one, pack_two = together(mixed, out_pair, pack_one, pack_two)
    pack_two = lax.all_gather(pack_two, "narrow", axis=0, tiled=False)

    mod_all = modulation.reshape(6, width)
    mixed_cat, out_all, branch_one, middle, second_low = call(
        functools.partial(middle_kernel, n),
        (quad_at, mixed, x_rows, mod_all, bout_full[None], out_quad, out_pair[0], out_two, out_pair[1]),
        [
            ((tokens, width), BF16),
            ((width, width), BF16),
            ((tokens, width), F32),
            ((tokens, width), F32),
            ((chips, tokens, width), BF16),
        ],
        scalars=1,
        name="middle",
        micros=5,
    )

    core_at = jnp.asarray(lax.axis_index("core"), jnp.int32).reshape(1)
    second_own = exchange(second_low, "chip")
    second_own, pack_two = together(second_own, pack_two)
    second_other = flip(second_own, "core", 1)
    side = ((chips, tokens, width), BF16)
    second_terms_own, second_terms_other, two_terms_own, two_terms_other, fc_terms, bfc1_terms = call(
        functools.partial(mlp_kernel, n),
        (second_own, second_other, two_own, two_other, pack_one, pack_two, bfc1_dev),
        [side, side, side, side, ((n, 2 * hidden_dev, width), BF16), ((8, hidden_all), F32)],
        [
            ((width, hidden_all), BF16),
            ((hidden_all, width), BF16),
            ((w * tokens, hidden_all), BF16),
            ((w * tokens, hidden_all), BF16),
            ((width, hidden_all), F32),
        ],
        name="mlp",
        micros=33,
    )
    bfc1_terms = bfc1_terms[0]
    fc_own = lax.psum_scatter(fc_terms, "narrow", scatter_dimension=0, tiled=False)
    second_got = exchange(core_add(second_terms_own, second_terms_other), "chip")
    chip = lax.axis_index("chip")
    two_came = flip(two_terms_other, "core", 1)
    two_sent = [
        (pick(two_terms_own, chip ^ r).astype(F32) + pick(two_came, chip ^ r).astype(F32)).astype(BF16)
        for r in range(chips)
    ]
    second_got, *two_sent = together(second_got, *two_sent)
    two_got = [two_sent[0]] + [flip(two_sent[r], "chip", r) for r in range(1, chips)]

    bfc2_terms = jnp.sum(grad_two.astype(F32), axis=0)

    grad_middle, grad_one, grad_mixed, middle_sums = call(
        functools.partial(middle_back_kernel, n),
        (second_got, middle, branch_one, grad_out, mod_all, out_all),
        [
            ((tokens, width), F32),
            ((tokens, width), BF16),
            ((n, tokens // n, width), BF16),
            ((4, width), F32),
        ],
        name="middle_back",
        micros=6,
    )
    grad_shift_two, grad_scale_two, grad_gate_one, bout_terms = middle_sums
    grad_mixed, fc_own = together(grad_mixed, fc_own)
    fc_all = lax.all_gather(fc_own, plane, axis=0, tiled=False)
    grad_mixed = exchange(grad_mixed, "narrow")
    piece = shard // w
    padded = -(-piece // 8) * 8
    wout_sides = call(
        functools.partial(wout_kernel, n),
        (core_at, mixed_cat, grad_one),
        [((chips, n * padded, width), BF16)] * 2,
        [((width, width), F32), ((2, chips, n, padded, width), BF16)],
        name="wout_terms",
        scalars=1,
        micros=4,
    )
    grad_mixed, wout_low = together(grad_mixed, core_add(*wout_sides))
    wout_got = exchange(wout_low, "chip")

    sent_cols = -(-3 * cols // LANES) * LANES
    wqkv_side = ((chips, n, padded, sent_cols), BF16)
    half_rows = ((n, tokens // 2, width), BF16)
    wqkv_own, wqkv_other, first_terms, last_terms, one_sums, projected_sums = call(
        functools.partial(attend_back_kernel, n, heads, score_scale),
        (core_at, projected, lse, grad_mixed, mixed_heads, unit_all, mod_one, qkv_wide),
        [wqkv_side, wqkv_side, half_rows, half_rows, ((8, width), F32), ((8, wide_cols), F32)],
        [
            ((image, wide_cols), BF16),
            ((image, heads * LANES), BF16),
            ((8, image), F32),
            ((image, width), BF16),
            ((width, sent_cols), F32),
            ((LANES, image), F32),
            ((2, chips, n, padded, sent_cols), BF16),
        ],
        name="attend_back",
        scalars=1,
        micros=38,
    )
    wqkv_own, wqkv_other, first_terms, fc_all, wout_got, *two_got = together(
        wqkv_own, wqkv_other, first_terms, fc_all, wout_got, *two_got
    )
    grad_shift_one = one_sums[0]
    grad_scale_one = one_sums[1]
    grad_first = lax.psum_scatter(first_terms, "narrow", scatter_dimension=0, tiled=False)
    wqkv_low, *two_got = together(core_add(wqkv_own, wqkv_other), *two_got)
    branch_two = bfc2_full[None] + sum(term.astype(F32) for term in two_got)
    wout_sum = add_up(wout_got).astype(BF16).reshape(n, padded, width)
    result = living * (middle + gate_two * branch_two)
    grad_gate_two = jnp.sum(grad_out * branch_two, axis=0)
    projected_sums = projected_sums[0].reshape(3, heads, LANES)[:, :, :head_size].reshape(3, cols)

    mod_terms = jnp.concatenate(
        [grad_shift_one, grad_scale_one, grad_gate_one, grad_shift_two, grad_scale_two, grad_gate_two]
    ).reshape(n, -1)
    qv_terms = jnp.zeros((2, n, cols), F32)
    qv_terms = lax.dynamic_update_slice(
        qv_terms, jnp.stack([projected_sums[0], projected_sums[2]])[:, None], (0, z, 0)
    )
    bfc1_wide = lax.dynamic_update_slice(
        jnp.zeros((n, w, hidden_dev), F32), bfc1_terms.reshape(n, 1, hidden_dev), (0, p, 0)
    )
    small_terms = jnp.concatenate(
        [
            mod_terms,
            qv_terms.reshape(n, -1),
            bout_terms.reshape(n, -1),
            bfc1_wide.reshape(n, -1),
            bfc2_terms.reshape(n, -1),
        ],
        axis=1,
    )
    wqkv_sum = add_up(exchange(wqkv_low, "chip")).astype(BF16)
    columns = sent_cols + width
    sent = jnp.concatenate([wqkv_sum, wout_sum], axis=2)
    extra = as_rows(small_terms, columns)
    got = exchange(jnp.concatenate([sent, extra], axis=1), "narrow")
    got, grad_first, fc_all, last_terms = together(got, grad_first, fc_all, last_terms)
    grad_last = lax.psum_scatter(last_terms, "narrow", scatter_dimension=0, tiled=False)
    grad_wfc1, grad_wfc2 = call(
        functools.partial(unpack_kernel, n),
        (fc_all,),
        [((shard, n * w * hidden_dev), F32), ((w * hidden_dev, width), F32)],
        name="unpack",
        micros=8,
    )
    grad_first = jnp.concatenate([grad_first, grad_last]).astype(F32)
    grad_input = grad_middle + norm_back(unit_one, inv_one, grad_first * (1.0 + scale_one))

    small_own = jnp.sum(from_rows(got[:, padded:], small_terms.shape[1]), axis=0)
    wout_own = add_up(got[:, :padded, sent_cols :]).astype(BF16)
    mod_size = mod_terms.shape[1]
    mod_low = small_own[:mod_size].astype(BF16)
    row = jnp.concatenate([small_own, cond_act[0]])
    parts = -(-width // (sent_cols))
    half = jnp.concatenate(jnp.split(wout_own, parts, axis=1))
    half = jnp.pad(half, ((0, 0), (0, sent_cols - width // parts)))
    sent = jnp.concatenate(
        [
            got[:, :padded, : sent_cols].reshape(n * padded, sent_cols),
            half,
            as_rows(row[None], sent_cols)[0],
        ]
    )
    got_own = share(sent, "chip")
    cond_part = dot(mod_low[None], w_ada, ((1,), (1,)))
    cond_total = jnp.sum(ring_gather(cond_part), axis=0)
    got_own, grad_wfc1, cond_total = together(got_own, grad_wfc1, cond_total)
    got_other = flip(got_own, "core", 1)
    got_other, grad_input = together(got_other, grad_input)
    rows = jnp.concatenate([part[:, (n + parts) * padded :] for part in (got_own, got_other)])
    shared = from_rows(rows, row.shape[0]).reshape(2, chips, -1)
    shared = jnp.where(core == 0, shared, shared[::-1]).transpose(1, 0, 2).reshape(w, -1)
    grad_wqkv, grad_wout = call(
        functools.partial(unpack_qkv_kernel, n, padded, cols),
        (core_at, got_own, got_other),
        [((shard, 3 * width), F32), ((shard, width), F32)],
        [(got_own.shape, BF16)] * 2 + [pltpu.SemaphoreType.DMA] * 2,
        scalars=1,
        space=pl.ANY,
        name="unpack_qkv",
        micros=4,
    )
    grad_condition = silu_pull(cond_total)[0]
    mod_rows = shared[:, :mod_size].astype(BF16)
    cond_rows = shared[:, small_own.shape[0] :].astype(BF16)
    grad_wada = dot(cond_rows, mod_rows, ((0,), (0,)))
    grad_bada = jnp.sum(mod_rows.astype(F32), axis=0)
    bias_sums = jnp.sum(shared[:, mod_size : small_own.shape[0]], axis=0)
    ends = [0]
    for piece in (qv_bias, b_out, b_fc1, b_fc2):
        ends.append(ends[-1] + piece.shape[0])
    grad_qv, grad_bout, grad_bfc1, grad_bfc2 = [
        bias_sums[low:high] for low, high in zip(ends[:-1], ends[1:])
    ]
    return (
        result[None],
        grad_input[None],
        grad_condition,
        grad_wada,
        grad_bada,
        grad_wqkv,
        grad_qv,
        grad_wout,
        grad_bout,
        grad_wfc1,
        grad_bfc1,
        grad_wfc2,
        grad_bfc2,
    )


def solution(mesh):
    narrow = mesh.shape["narrow"]
    mesh = Mesh(mesh.devices.reshape(-1, 2, narrow), ("chip", "core", "narrow"))
    in_specs = (
        P(WIDE, "narrow", None),
        P(WIDE, None),
        P(WIDE),
        P(None, "narrow"),
        P("narrow"),
        P("narrow", None),
        P("narrow"),
        P("narrow", None),
        P("narrow"),
        P("narrow", None),
        P("narrow"),
        P("narrow", None),
        P("narrow"),
        P(WIDE, "narrow", None),
    )
    out_specs = (
        P(WIDE, "narrow", None),
        P(WIDE, "narrow", None),
        P(WIDE, None),
        P(None, "narrow"),
        P("narrow"),
        P("narrow", None),
        P("narrow"),
        P("narrow", None),
        P("narrow"),
        P("narrow", None),
        P("narrow"),
        P("narrow", None),
        P("narrow"),
    )
    return jax.shard_map(
        per_device, mesh=mesh, in_specs=in_specs, out_specs=out_specs, check_vma=False
    )
```

```python
import functools
import math

import jax
import jax.numpy as jnp
from jax import lax
from jax.experimental import pallas as pl
from jax.experimental.pallas import tpu as pltpu
from jax.sharding import Mesh
from jax.sharding import PartitionSpec as P

HEADS = 16
WIDE = ("chip", "core")
F32 = jnp.float32
BF16 = jnp.bfloat16
LANES = 128
ROOT = math.sqrt(2 / math.pi)
LOG2E = math.log2(math.e)


def dot(left, right, dims=((1,), (0,))):
    return lax.dot_general(left, right, (dims, ((), ())), preferred_element_type=F32)


def flip(block, axis, bit):
    size = lax.axis_size(axis)
    return lax.ppermute(block, axis, [(i, i ^ bit) for i in range(size)])


def exchange(blocks, axis):
    return lax.all_to_all(blocks, axis, 0, 0, tiled=False)


def share(block, axis):
    return exchange(jnp.broadcast_to(block[None], (lax.axis_size(axis),) + block.shape), axis)


def ring(block, step):
    n = lax.axis_size("narrow")
    return lax.ppermute(block, "narrow", [(i, (i + step) % n) for i in range(n)])


def pick(blocks, index):
    return lax.dynamic_index_in_dim(blocks, index, 0, keepdims=False)


def together(*values):
    return lax.optimization_barrier(values)


def add_up(blocks):
    return sum(blocks[i].astype(F32) for i in range(blocks.shape[0]))


def place(blocks, index_of):
    buffer = jnp.zeros((len(blocks),) + blocks[0].shape, blocks[0].dtype)
    for j, block in enumerate(blocks):
        buffer = lax.dynamic_update_index_in_dim(buffer, block, index_of(j), 0)
    return buffer


def ring_gather(block):
    n = lax.axis_size("narrow")
    z = lax.axis_index("narrow")
    blocks = [block] + [ring(block, j) for j in range(1, n)]
    return place(blocks, lambda j: lax.rem(z + n - j, n))


def as_rows(values, columns):
    rows = -(-values.shape[1] // (4 * columns)) * 4
    values = jnp.pad(values, ((0, 0), (0, rows * columns - values.shape[1])))
    high = values.astype(BF16)
    low = (values - high.astype(F32)).astype(BF16)
    return jnp.concatenate([part.reshape(-1, rows, columns) for part in (high, low)], axis=1)


def from_rows(rows, size):
    half = rows.shape[1] // 2
    total = rows[:, :half].astype(F32) + rows[:, half:].astype(F32)
    return total.reshape(rows.shape[0], -1)[:, :size]


def whole_lanes(row):
    return jnp.pad(row, (0, -row.shape[0] % LANES))


def core_add(own, other):
    return (own.astype(F32) + flip(other, "core", 1).astype(F32)).astype(BF16)


def call(kernel, args, outs, scratch=(), scalars=0, name=None, micros=1, space=pltpu.VMEM):
    vmem = pl.BlockSpec(memory_space=pltpu.VMEM)
    given = pl.BlockSpec(memory_space=space)
    smem = pl.BlockSpec(memory_space=pltpu.SMEM)
    return pl.pallas_call(
        kernel,
        out_shape=tuple(jax.ShapeDtypeStruct(shape, dtype) for shape, dtype in outs),
        in_specs=[smem if i < scalars else given for i in range(len(args))],
        out_specs=tuple(vmem for _ in outs),
        scratch_shapes=[
            part if isinstance(part, pltpu.SemaphoreType) else pltpu.VMEM(*part) for part in scratch
        ],
        compiler_params=pltpu.CompilerParams(vmem_limit_bytes=56 << 20),
        cost_estimate=pl.CostEstimate(
            flops=1000000000 * micros, bytes_accessed=3000000 * micros, transcendentals=0
        ),
        name=name,
    )(*args)


def pack_kernel(n, w, p_ref, fc1_ref, fc2_ref, first_ref, second_ref):
    shard = fc1_ref.shape[0]
    rows = fc2_ref.shape[0] // w
    full = fc2_ref.shape[0]
    for q in range(w):

        @pl.when(p_ref[0] == q)
        def _(q=q):
            second_ref[...] = fc2_ref[q * rows : (q + 1) * rows]
            pieces = [
                fc1_ref[part : part + rows, a * full + q * rows : a * full + (q + 1) * rows]
                for part in range(0, shard, rows)
                for a in range(n)
            ]
            first_ref[...] = jnp.concatenate(pieces, axis=1)


def qkv_kernel(n, w, place_ref, w_ref, out_ref):
    padded, sent = out_ref.shape[1:]
    piece = w_ref.shape[0] // w
    width = w_ref.shape[1] // 3
    cols = width // n
    for q in range(w):

        @pl.when(place_ref[0] == q)
        def _(q=q):
            for a in range(n):
                block = jnp.concatenate(
                    [
                        w_ref[q * piece : (q + 1) * piece, t * width + a * cols : t * width + (a + 1) * cols]
                        for t in range(3)
                    ],
                    axis=1,
                )
                if sent > 3 * cols:
                    fill = jnp.zeros((piece, sent - 3 * cols), BF16)
                    block = jnp.concatenate([block, fill], axis=1)
                if padded > piece:
                    fill = jnp.zeros((padded - piece, sent), BF16)
                    block = jnp.concatenate([block, fill], axis=0)
                out_ref[a] = block


def qkv_join_kernel(n, heads, padded, core_ref, own_ref, other_ref, wide_ref, joined):
    chips = own_ref.shape[0]
    width = wide_ref.shape[0]
    piece = width // (n * 2 * chips)
    size = width // (n * heads)
    for core in range(2):

        @pl.when(core_ref[0] == core)
        def _(core=core):
            for q in range(2 * chips):
                got_ref = own_ref if q % 2 == core else other_ref
                for a in range(n):
                    at = (a * 2 * chips + q) * piece
                    joined[at : at + piece] = got_ref[q // 2, a * padded : a * padded + piece]

    pad = jnp.zeros((width, LANES - size), BF16)
    for t in range(3 * heads):
        wide_ref[:, t * LANES : (t + 1) * LANES] = jnp.concatenate(
            [joined[:, t * size : (t + 1) * size], pad], axis=1
        )


def attend_kernel(
    n, heads, scale, unit_ref, mod_ref, wide_ref, bias_ref, mixed_ref, proj_ref, lse_ref, mixed_wide
):
    width = unit_ref.shape[2]
    image = proj_ref.shape[0]
    tokens = image // n
    size = width // (n * heads)
    pad_row = jnp.zeros((1, LANES - size), F32)
    bias = []
    for t in range(3 * heads):
        bias += [bias_ref[:, t * size : (t + 1) * size], pad_row]
    bias = jnp.concatenate(bias, axis=1)
    gain = 1.0 + mod_ref[1:2]
    shift = mod_ref[0:1]

    def project(i, carry):
        rows = pl.ds(pl.multiple_of(i * 2 * tokens, 2 * tokens), 2 * tokens)
        both = jnp.concatenate([unit_ref[2 * i, :tokens], unit_ref[2 * i + 1, :tokens]], axis=0)
        first = (both.astype(F32) * gain + shift).astype(BF16)
        proj_ref[rows] = (dot(first, wide_ref[...]) + bias).astype(BF16)
        return carry

    lax.fori_loop(0, n // 2, project, 0)

    def head(h, carry):
        at = lambda t: pl.ds(pl.multiple_of((t * heads + h) * LANES, LANES), LANES)
        keys = proj_ref[:, at(1)]
        values_t = proj_ref[:, at(2)].T

        def block(i, carry):
            rows = pl.ds(pl.multiple_of(i * 4 * tokens, 4 * tokens), 4 * tokens)
            scores = dot(keys, proj_ref[rows, at(0)], ((1,), (1,)))
            top = jnp.max(scores, axis=0, keepdims=True)
            grown = jnp.exp2((scores - top) * (scale * LOG2E))
            total = jnp.sum(grown, axis=0, keepdims=True)
            mixed = dot(values_t, grown.astype(BF16)) / total
            mixed = mixed.T.astype(BF16)
            for k in range(4):
                mixed_wide[4 * i + k, h] = mixed[k * tokens : (k + 1) * tokens]
            lse_ref[h, :, rows] = top * (scale * LOG2E) + jnp.log2(total)
            return carry

        return lax.fori_loop(0, n // 4, block, carry)

    lax.fori_loop(0, heads, head, 0)

    def join(i, carry):
        rows = tokens // n
        mixed_ref[i] = jnp.concatenate(
            [
                mixed_wide[i, h, q * rows : (q + 1) * rows, :size]
                for q in range(n)
                for h in range(heads)
            ],
            axis=1,
        )
        return carry

    lax.fori_loop(0, n, join, 0)


def attend_back_kernel(
    n,
    heads,
    scale,
    core_ref,
    proj_ref,
    lse_ref,
    grad_ref,
    mixed_ref,
    unit_ref,
    mod_ref,
    wide_ref,
    *rest,
):
    terms_own_ref, terms_other_ref, first_ref, last_ref, sums_ref, proj_sums_ref = rest[:6]
    grad_proj, grad_wide, delta_ref, first_low, terms, query_acc, terms_low = rest[6:]
    width = unit_ref.shape[2]
    image = proj_ref.shape[0]
    tokens = image // n
    cols = grad_ref.shape[2] // n
    size = cols // heads
    pad = jnp.zeros((tokens, LANES - size), BF16)
    ones = jnp.ones((8, LANES), F32)
    gain = 1.0 + mod_ref[1:2]
    shift = mod_ref[0:1]

    def prepare(i, carry):
        rows = pl.ds(pl.multiple_of(i * tokens, tokens), tokens)
        for h in range(heads):
            lanes = [slice(q * cols + h * size, q * cols + (h + 1) * size) for q in range(n)]
            grad = jnp.concatenate([grad_ref[i, :, at] for at in lanes], axis=0)
            mixed = jnp.concatenate([mixed_ref[i, :, at] for at in lanes], axis=0)
            grad = jnp.concatenate([grad, pad], axis=1)
            mixed = jnp.concatenate([mixed, pad], axis=1)
            grad_wide[rows, h * LANES : (h + 1) * LANES] = grad
            both = grad.astype(F32) * mixed.astype(F32)
            delta = lax.dot_general(
                ones, both, (((1,), (1,)), ((), ())),
                preferred_element_type=F32, precision=lax.Precision.HIGHEST,
            )
            delta_ref[h, :, rows] = delta[0:1]
        first_low[rows] = (unit_ref[i, :tokens].astype(F32) * gain + shift).astype(BF16)
        return carry

    lax.fori_loop(0, n, prepare, 0)

    def head(h, carry):
        q_at, k_at, v_at = [
            pl.ds(pl.multiple_of((t * heads + h) * LANES, LANES), LANES) for t in range(3)
        ]
        query_acc[...] = jnp.zeros_like(query_acc)

        def block(j, carry):
            rows = pl.ds(pl.multiple_of(j * 4 * tokens, 4 * tokens), 4 * tokens)
            keys = proj_ref[rows, k_at]
            values = proj_ref[rows, v_at]
            queries = proj_ref[:, q_at]
            grads = grad_wide[:, q_at]
            weights = jnp.exp2(dot(keys, queries, ((1,), (1,))) * (scale * LOG2E) - lse_ref[h])
            grad_weights = dot(values, grads, ((1,), (1,)))
            grad_scores = (weights * (grad_weights - delta_ref[h])).astype(BF16)
            grad_proj[rows, v_at] = dot(weights.astype(BF16), grads).astype(BF16)
            grad_proj[rows, k_at] = (dot(grad_scores, queries) * scale).astype(BF16)
            query_acc[...] += dot(keys.T, grad_scores)
            return carry

        carry = lax.fori_loop(0, n // 4, block, carry)
        grad_proj[:, q_at] = (query_acc[...] * scale).T.astype(BF16)
        return carry

    lax.fori_loop(0, heads, head, 0)
    proj_sums_ref[...] = jnp.zeros_like(proj_sums_ref)
    sums_ref[...] = jnp.zeros_like(sums_ref)

    def out(i, carry):
        rows = pl.ds(pl.multiple_of(i * 2 * tokens, 2 * tokens), 2 * tokens)
        block = grad_proj[rows]
        grad = dot(block, wide_ref[...], ((1,), (1,)))
        proj_sums_ref[0:1] += jnp.sum(block.astype(F32), axis=0, keepdims=True)
        sums_ref[0:1] += jnp.sum(grad, axis=0, keepdims=True)
        for k in range(2):
            part = grad[k * tokens : (k + 1) * tokens]
            unit = unit_ref[2 * i + k, :tokens].astype(F32)
            sums_ref[1:2] += jnp.sum(part * unit, axis=0, keepdims=True)
            first_ref[2 * i + k] = part[: tokens // 2].astype(BF16)
            last_ref[2 * i + k] = part[tokens // 2 :].astype(BF16)
        return carry

    lax.fori_loop(0, n // 2, out, 0)

    def third(t, carry):
        lanes = pl.ds(pl.multiple_of(t * heads * LANES, LANES), heads * LANES)
        part = dot(first_low[...], grad_proj[:, lanes], ((0,), (0,)))
        terms[t] = jnp.concatenate(
            [part[:, h * LANES : h * LANES + size] for h in range(heads)], axis=1
        ).astype(BF16)
        return carry

    lax.fori_loop(0, 3, third, 0)
    _, chips, _, padded, sent = terms_low.shape

    def get(rows):
        parts = [terms[t, rows] for t in range(3)]
        if sent > 3 * cols:
            parts.append(jnp.zeros((parts[0].shape[0], sent - 3 * cols), BF16))
        return jnp.concatenate(parts, axis=1)

    def store(q, a, block):
        terms_low[q % 2, q // 2, a] = block

    to_pieces(get, store, n, width // n, 2 * chips, padded)
    terms_own_ref[...] = terms_low[core_ref[0]]
    terms_other_ref[...] = terms_low[1 - core_ref[0]]


def to_pieces(get, store, n, shard, w, padded):
    piece = shard // w
    for a in range(n):
        for q in range(w):
            at = a * shard + q * piece
            block = get(slice(at, at + piece))
            if padded > piece:
                fill = jnp.zeros((padded - piece, block.shape[1]), BF16)
                block = jnp.concatenate([block, fill], axis=0)
            store(q, a, block)


def wout_kernel(n, core_ref, mixed_ref, grad_ref, own_ref, other_ref, terms, low):
    step = grad_ref.shape[1] // 3

    def third(t, carry):
        lanes = pl.ds(pl.multiple_of(t * step, LANES), step)
        terms[:, lanes] = dot(mixed_ref[...], grad_ref[:, lanes], ((0,), (0,))).astype(BF16)
        return carry

    lax.fori_loop(0, 3, third, 0)
    _, chips, _, padded, _ = low.shape

    def store(q, a, block):
        low[q % 2, q // 2, a] = block

    to_pieces(lambda rows: terms[rows], store, n, terms.shape[0] // n, 2 * chips, padded)
    for a in range(n):
        own_ref[:, a * padded : (a + 1) * padded] = low[core_ref[0], :, a]
        other_ref[:, a * padded : (a + 1) * padded] = low[1 - core_ref[0], :, a]


def middle_kernel(
    n,
    core_ref,
    got_ref,
    x_ref,
    mod_ref,
    bias_ref,
    own_ref,
    other_ref,
    mixed_ref,
    out_ref,
    branch_ref,
    middle_ref,
    second_ref,
):
    rows = got_ref.shape[1]
    cols = got_ref.shape[2] // n
    chips = own_ref.shape[0]
    piece = out_ref.shape[0] // (n * 2 * chips)
    for core in range(2):

        @pl.when(core_ref[0] == core)
        def _(core=core):
            for q in range(2 * chips):
                part_ref = own_ref if q % 2 == core else other_ref
                for a in range(n):
                    at = (a * 2 * chips + q) * piece
                    out_ref[at : at + piece] = part_ref[q // 2, a, :piece]

    for q in range(n):
        mixed_ref[q * rows : (q + 1) * rows] = jnp.concatenate(
            [got_ref[j, :, q * cols : (q + 1) * cols] for j in range(n)], axis=1
        )
    branch = dot(mixed_ref[...], out_ref[...]) + bias_ref[...]
    middle = x_ref[...] + mod_ref[2:3] * branch
    unit, _ = norm_parts(middle)
    branch_ref[...] = branch
    middle_ref[...] = middle
    second = (unit * (1.0 + mod_ref[4:5]) + mod_ref[3:4]).astype(BF16)
    for k in range(second_ref.shape[0]):
        second_ref[k] = second


def middle_back_kernel(
    n, came_ref, middle_ref, branch_ref, d_out_ref, mod_ref, out_ref, *rest
):
    grad_middle_ref, grad_one_ref, mixed_ref, sums_ref = rest
    rows = mixed_ref.shape[1]
    cols = mixed_ref.shape[2] // n
    unit, inv = norm_parts(middle_ref[...])
    grad_second = came_ref[0].astype(F32)
    for r in range(1, came_ref.shape[0]):
        grad_second += came_ref[r].astype(F32)
    grad_middle = d_out_ref[...] + norm_back(unit, inv, grad_second * (1.0 + mod_ref[4:5]))
    grad_one = (mod_ref[2:3] * grad_middle).astype(BF16)
    grad_middle_ref[...] = grad_middle
    grad_one_ref[...] = grad_one
    parts = (grad_second, grad_second * unit, grad_middle * branch_ref[...], grad_one.astype(F32))
    for k, part in enumerate(parts):
        sums_ref[k : k + 1] = jnp.sum(part, axis=0, keepdims=True)
    mixed = dot(grad_one, out_ref[...], ((1,), (1,))).astype(BF16)
    for j in range(n):
        mixed_ref[j] = jnp.concatenate(
            [mixed[q * rows : (q + 1) * rows, j * cols : (j + 1) * cols] for q in range(n)], axis=1
        )


def mlp_kernel(
    n,
    own_ref,
    other_ref,
    two_own_ref,
    two_other_ref,
    pack_one_ref,
    pack_two_ref,
    bias_ref,
    second_own_ref,
    second_other_ref,
    two_sum_own_ref,
    two_sum_other_ref,
    grad_ref,
    bias_grad_ref,
    fc1,
    fc2,
    active_all,
    hidden_all,
    grad_fc1,
):
    chips, tokens, width = own_ref.shape
    rows = pack_one_ref.shape[1]
    units = n * rows
    halves = width // units
    for a in range(n):
        fc2[a * rows : (a + 1) * rows] = pack_two_ref[a]
        for part in range(halves):
            at = (a * halves + part) * rows
            fc1[at : at + rows] = pack_one_ref[a, :, part * units : (part + 1) * units]
    bias_grad_ref[...] = jnp.zeros_like(bias_grad_ref)
    sides = (
        (own_ref, two_own_ref, second_own_ref, two_sum_own_ref),
        (other_ref, two_other_ref, second_other_ref, two_sum_other_ref),
    )
    for side, refs in enumerate(sides):

        def block(i, carry, side=side, refs=refs):
            x_ref, g_ref, second_ref, two_ref = refs
            at = pl.ds(pl.multiple_of(side * chips * tokens + i * 2 * tokens, 2 * tokens), 2 * tokens)
            some = pl.ds(2 * i, 2)
            rows_x = x_ref[some].reshape(2 * tokens, width)
            rows_g = g_ref[some].reshape(2 * tokens, width)
            hidden = dot(rows_x, fc1[...]) + bias_ref[...]
            square = hidden * hidden
            inner = ROOT * (hidden + 0.044715 * square * hidden)
            bend = jnp.tanh(inner)
            half = 0.5 * (1.0 + bend)
            active = (hidden * half).astype(BF16)
            slope = half + 0.5 * hidden * (1.0 - bend * bend) * (ROOT * (1.0 + 3 * 0.044715 * square))
            grad = (dot(rows_g, fc2[...], ((1,), (1,))) * slope).astype(BF16)
            active_all[at] = active
            hidden_all[at] = grad
            second = dot(grad, fc1[...], ((1,), (1,))).astype(BF16)
            second_ref[some] = second.reshape(2, tokens, width)
            two_ref[some] = dot(active, fc2[...]).astype(BF16).reshape(2, tokens, width)
            bias_grad_ref[0:1] += jnp.sum(grad.astype(F32), axis=0, keepdims=True)
            return carry

        lax.fori_loop(0, chips // 2, block, 0)
    step = width // 3
    half_rows = chips * tokens

    def third(t, carry):
        lanes = pl.ds(pl.multiple_of(t * step, LANES), step)
        part = dot(
            active_all[:half_rows], two_own_ref[:, :, lanes].reshape(half_rows, step), ((0,), (0,))
        ) + dot(
            active_all[half_rows:], two_other_ref[:, :, lanes].reshape(half_rows, step), ((0,), (0,))
        )
        for a in range(n):
            grad_ref[a, :rows, lanes] = part[a * rows : (a + 1) * rows].astype(BF16)
        grad_fc1[lanes] = (
            dot(own_ref[:, :, lanes].reshape(half_rows, step), hidden_all[:half_rows], ((0,), (0,)))
            + dot(other_ref[:, :, lanes].reshape(half_rows, step), hidden_all[half_rows:], ((0,), (0,)))
        ).astype(BF16)
        return carry

    lax.fori_loop(0, 3, third, 0)
    for a in range(n):
        grad_ref[a, rows:] = jnp.concatenate(
            [
                grad_fc1[(a * halves + part) * rows : (a * halves + part + 1) * rows]
                for part in range(halves)
            ],
            axis=1,
        )


def unpack_kernel(n, got_ref, fc1_ref, fc2_ref):
    w, _, width = got_ref.shape
    rows = got_ref.shape[1] // 2
    units = n * rows
    full = w * rows
    for q in range(w):
        fc2_ref[q * rows : (q + 1) * rows] = got_ref[q, :rows].astype(F32)
    for part in range(width // units):
        for a in range(n):
            at = part * units + a * rows
            fc1_ref[part * rows : (part + 1) * rows, a * full : (a + 1) * full] = jnp.concatenate(
                [got_ref[q, rows:, at : at + rows].astype(F32) for q in range(w)], axis=1
            )


def finish_kernel(
    n,
    padded,
    cols,
    core_ref,
    own_from,
    other_from,
    wqkv_ref,
    wout_ref,
    wada_ref,
    bada_ref,
    *rest,
):
    bias_refs, (own_ref, other_ref, rows_ref, own_sem, other_sem) = rest[:-5], rest[-5:]
    own_copy = pltpu.make_async_copy(own_from, own_ref, own_sem)
    other_copy = pltpu.make_async_copy(other_from, other_ref, other_sem)
    own_copy.start()
    other_copy.start()
    own_copy.wait()
    other_copy.wait()
    chips, _, sent = own_ref.shape
    piece = wqkv_ref.shape[0] // (2 * chips)
    parts = -(-wout_ref.shape[1] // sent)
    part = wout_ref.shape[1] // parts
    base = (n + parts) * padded
    half = (own_ref.shape[1] - base) // 2
    for core in range(2):

        @pl.when(core_ref[0] == core)
        def _(core=core):
            for q in range(2 * chips):
                got_ref = own_ref if q % 2 == core else other_ref
                wqkv_ref[q * piece : (q + 1) * piece] = jnp.concatenate(
                    [
                        got_ref[q // 2, a * padded : a * padded + piece, t * cols : (t + 1) * cols]
                        .astype(F32)
                        for t in range(3)
                        for a in range(n)
                    ],
                    axis=1,
                )
                wout_ref[q * piece : (q + 1) * piece] = jnp.concatenate(
                    [
                        got_ref[q // 2, a * padded : a * padded + piece, :part].astype(F32)
                        for a in range(n, n + parts)
                    ],
                    axis=1,
                )
                small = got_ref[q // 2, base : base + half].astype(F32)
                small += got_ref[q // 2, base + half : base + 2 * half].astype(F32)
                rows_ref[q : q + 1] = jnp.concatenate(
                    [small[r : r + 1] for r in range(half)], axis=1
                )

    size, width = wada_ref.shape
    at = -(-size // LANES) * LANES
    mod = rows_ref[:, :size].astype(BF16)
    cond = rows_ref[:, at : at + width].astype(BF16)
    wada_ref[...] = dot(mod, cond, ((0,), (0,)))
    bada_ref[...] = jnp.sum(mod.astype(F32), axis=0)
    at += -(-width // LANES) * LANES
    for bias_ref in bias_refs:
        bias_ref[...] = jnp.sum(rows_ref[:, at : at + bias_ref.shape[0]], axis=0)
        at += bias_ref.shape[0]


def rows_mean(rows_in):
    return jnp.mean(rows_in, axis=-1, keepdims=True)


def norm_parts(rows_in):
    centered = rows_in - rows_mean(rows_in)
    inv = lax.rsqrt(rows_mean(centered * centered) + 1e-06)
    return centered * inv, inv


def norm_back(unit, inv, grad_unit):
    return inv * (grad_unit - rows_mean(grad_unit) - unit * rows_mean(grad_unit * unit))


def per_device(
    x_input,
    condition,
    counts,
    w_ada,
    b_ada,
    w_qkv,
    qv_bias,
    w_out,
    b_out,
    w_fc1,
    b_fc1,
    w_fc2,
    b_fc2,
    d_out,
):
    n = lax.axis_size("narrow")
    chips = lax.axis_size("chip")
    w = 2 * chips
    z = lax.axis_index("narrow")
    p = 2 * lax.axis_index("chip") + lax.axis_index("core")
    plane = ("chip", "core")
    slot_count, tokens, width = x_input.shape
    x_rows = x_input.reshape(tokens, width)
    heads = HEADS // n
    head_size = width // HEADS
    score_scale = head_size ** (-0.5)
    shard = width // n
    sub = shard // 4
    hidden_dev = w_fc2.shape[0] // w
    hidden_all = n * hidden_dev
    cols = heads * head_size
    image = n * tokens

    living = (counts[0] > 0).astype(F32)

    piece = shard // w
    padded = -(-piece // 8) * 8
    sent_cols = -(-3 * cols // LANES) * LANES
    wide_cols = 3 * heads * LANES
    core = lax.axis_index("core")
    core_at = jnp.asarray(core, jnp.int32).reshape(1)
    plane_at = jnp.asarray(p, jnp.int32).reshape(1)
    (qkv_to,) = call(
        functools.partial(qkv_kernel, n, w),
        (plane_at, w_qkv),
        [((n, padded, sent_cols), BF16)],
        scalars=1,
        name="qkv_to",
        micros=3,
    )
    qkv_got = exchange(qkv_to, "narrow").reshape(n * padded, sent_cols)
    qkv_own = share(qkv_got, "chip")
    (qkv_wide,) = call(
        functools.partial(qkv_join_kernel, n, heads, padded),
        (core_at, qkv_own, flip(qkv_own, "core", 1)),
        [((width, wide_cols), BF16)],
        [((width, sent_cols), BF16)],
        scalars=1,
        name="qkv_join",
        micros=4,
    )

    cond_act, silu_pull = jax.vjp(jax.nn.silu, condition)
    cond_low = cond_act.astype(BF16)
    x_rows, qkv_to = together(x_rows, qkv_to)
    unit_one, inv_one = norm_parts(x_rows)
    unit_low, cond_low = together(unit_one.astype(BF16), cond_low)
    out_mine = lax.dynamic_slice_in_dim(w_out, p * piece, piece, 0)
    out_mine = jnp.pad(out_mine, ((0, padded - piece), (0, 0)))
    unit_all = lax.all_gather(
        jnp.concatenate([unit_low, out_mine]), "narrow", axis=0, tiled=False
    )
    mod_part = dot(cond_low, w_ada)[0] + b_ada.astype(F32)
    small = jnp.concatenate([mod_part] + [v.astype(F32) for v in (qv_bias, b_out, b_fc1, b_fc2)])
    small_all = ring_gather(small)
    ends = [0]
    for piece in (mod_part, qv_bias, b_out, b_fc1, b_fc2):
        ends.append(ends[-1] + piece.shape[0])
    modulation, qv_full, bout_full, bfc1_full, bfc2_full = [
        small_all[:, low:high].reshape(-1) for low, high in zip(ends[:-1], ends[1:])
    ]
    shift_one, scale_one, gate_one, shift_two, scale_two, gate_two = [
        modulation[None, k * width : (k + 1) * width] for k in range(6)
    ]


    pack_one, pack_two = call(
        functools.partial(pack_kernel, n, w),
        (jnp.asarray(p, jnp.int32).reshape(1), w_fc1, w_fc2),
        [((hidden_dev, width), BF16)] * 2,
        scalars=1,
        name="pack",
        micros=3,
    )

    grad_out = living * d_out.reshape(tokens, width)
    grad_two = (gate_two * grad_out).astype(BF16)
    two_own = share(grad_two, "chip")
    unit_all, pack_one = together(unit_all, pack_one)
    out_own = share(unit_all[:, tokens:], "chip")
    pack_one = lax.all_gather(pack_one, "narrow", axis=0, tiled=False)
    bfc1_dev = lax.dynamic_index_in_dim(bfc1_full.reshape(n, w, hidden_dev), p, 1, keepdims=False)
    bfc1_dev = bfc1_dev.reshape(1, hidden_all)

    qv_two = qv_full.reshape(2, n, cols)
    q_bias = lax.dynamic_index_in_dim(qv_two[0], z, 0, keepdims=True)
    v_bias = lax.dynamic_index_in_dim(qv_two[1], z, 0, keepdims=True)
    bias_three = jnp.concatenate([q_bias, jnp.zeros_like(q_bias), v_bias], axis=1)
    mod_one = jnp.concatenate([shift_one, scale_one], axis=0)
    mixed, projected, lse = call(
        functools.partial(attend_kernel, n, heads, score_scale),
        (unit_all, mod_one, qkv_wide, bias_three),
        [
            ((n, tokens // n, width), BF16),
            ((image, wide_cols), BF16),
            ((heads, 1, image), F32),
        ],
        [((n, heads, tokens, LANES), BF16)],
        name="attend",
        micros=26,
    )
    mixed, two_own, out_own = together(mixed, two_own, out_own)
    two_other = flip(two_own, "core", 1)
    mixed_heads = mixed
    out_other = flip(out_own, "core", 1)
    mixed = exchange(mixed, "narrow")
    mixed, out_other, pack_one, pack_two = together(mixed, out_other, pack_one, pack_two)
    pack_two = lax.all_gather(pack_two, "narrow", axis=0, tiled=False)

    mod_all = modulation.reshape(6, width)
    mixed_cat, out_all, branch_one, middle, second_low = call(
        functools.partial(middle_kernel, n),
        (core_at, mixed, x_rows, mod_all, bout_full[None], out_own, out_other),
        [
            ((tokens, width), BF16),
            ((width, width), BF16),
            ((tokens, width), F32),
            ((tokens, width), F32),
            ((chips, tokens, width), BF16),
        ],
        scalars=1,
        name="middle",
        micros=5,
    )

    second_own = exchange(second_low, "chip")
    second_own, pack_two = together(second_own, pack_two)
    second_other = flip(second_own, "core", 1)
    side = ((chips, tokens, width), BF16)
    second_terms_own, second_terms_other, two_terms_own, two_terms_other, fc_terms, bfc1_terms = call(
        functools.partial(mlp_kernel, n),
        (second_own, second_other, two_own, two_other, pack_one, pack_two, bfc1_dev),
        [side, side, side, side, ((n, 2 * hidden_dev, width), BF16), ((8, hidden_all), F32)],
        [
            ((width, hidden_all), BF16),
            ((hidden_all, width), BF16),
            ((w * tokens, hidden_all), BF16),
            ((w * tokens, hidden_all), BF16),
            ((width, hidden_all), BF16),
        ],
        name="mlp",
        micros=33,
    )
    bfc1_terms = bfc1_terms[0]
    fc_own = lax.psum_scatter(fc_terms, "narrow", scatter_dimension=0, tiled=False)
    second_got = exchange(core_add(second_terms_own, second_terms_other), "chip")
    chip = lax.axis_index("chip")
    two_came = flip(two_terms_other, "core", 1)
    two_sent = [
        (pick(two_terms_own, chip ^ r).astype(F32) + pick(two_came, chip ^ r).astype(F32)).astype(BF16)
        for r in range(chips)
    ]
    second_got, *two_sent = together(second_got, *two_sent)
    two_got = [two_sent[0]] + [flip(two_sent[r], "chip", r) for r in range(1, chips)]

    bfc2_terms = jnp.sum(grad_two.astype(F32), axis=0)

    grad_middle, grad_one, grad_mixed, middle_sums = call(
        functools.partial(middle_back_kernel, n),
        (second_got, middle, branch_one, grad_out, mod_all, out_all),
        [
            ((tokens, width), F32),
            ((tokens, width), BF16),
            ((n, tokens // n, width), BF16),
            ((4, width), F32),
        ],
        name="middle_back",
        micros=6,
    )
    grad_shift_two, grad_scale_two, grad_gate_one, bout_terms = middle_sums
    grad_mixed, fc_own = together(grad_mixed, fc_own)
    fc_all = lax.all_gather(fc_own, plane, axis=0, tiled=False)
    grad_mixed = exchange(grad_mixed, "narrow")
    wout_sides = call(
        functools.partial(wout_kernel, n),
        (core_at, mixed_cat, grad_one),
        [((chips, n * padded, width), BF16)] * 2,
        [((width, width), BF16), ((2, chips, n, padded, width), BF16)],
        name="wout_terms",
        scalars=1,
        micros=4,
    )
    grad_mixed, wout_low = together(grad_mixed, core_add(*wout_sides))
    wout_got = exchange(wout_low, "chip")

    wqkv_side = ((chips, n, padded, sent_cols), BF16)
    half_rows = ((n, tokens // 2, width), BF16)
    wqkv_own, wqkv_other, first_terms, last_terms, one_sums, projected_sums = call(
        functools.partial(attend_back_kernel, n, heads, score_scale),
        (core_at, projected, lse, grad_mixed, mixed_heads, unit_all, mod_one, qkv_wide),
        [wqkv_side, wqkv_side, half_rows, half_rows, ((8, width), F32), ((8, wide_cols), F32)],
        [
            ((image, wide_cols), BF16),
            ((image, heads * LANES), BF16),
            ((heads, 1, image), F32),
            ((image, width), BF16),
            ((3, width, cols), BF16),
            ((LANES, image), F32),
            ((2, chips, n, padded, sent_cols), BF16),
        ],
        name="attend_back",
        scalars=1,
        micros=38,
    )
    wqkv_own, wqkv_other, first_terms, fc_all, wout_got, *two_got = together(
        wqkv_own, wqkv_other, first_terms, fc_all, wout_got, *two_got
    )
    grad_shift_one = one_sums[0]
    grad_scale_one = one_sums[1]
    wout_sum = add_up(wout_got).astype(BF16).reshape(n, padded, width)
    first_terms = jnp.concatenate([first_terms, wout_sum], axis=1)
    grad_first = lax.psum_scatter(first_terms, "narrow", scatter_dimension=0, tiled=False)
    wqkv_low, *two_got = together(core_add(wqkv_own, wqkv_other), *two_got)
    branch_two = bfc2_full[None] + sum(term.astype(F32) for term in two_got)
    result = living * (middle + gate_two * branch_two)
    grad_gate_two = jnp.sum(grad_out * branch_two, axis=0)
    projected_sums = projected_sums[0].reshape(3, heads, LANES)[:, :, :head_size].reshape(3, cols)

    mod_terms = jnp.concatenate(
        [grad_shift_one, grad_scale_one, grad_gate_one, grad_shift_two, grad_scale_two, grad_gate_two]
    ).reshape(n, -1)
    qv_terms = jnp.zeros((2, n, cols), F32)
    qv_terms = lax.dynamic_update_slice(
        qv_terms, jnp.stack([projected_sums[0], projected_sums[2]])[:, None], (0, z, 0)
    )
    bfc1_wide = lax.dynamic_update_slice(
        jnp.zeros((n, w, hidden_dev), F32), bfc1_terms.reshape(n, 1, hidden_dev), (0, p, 0)
    )
    small_terms = jnp.concatenate(
        [
            mod_terms,
            qv_terms.reshape(n, -1),
            bout_terms.reshape(n, -1),
            bfc1_wide.reshape(n, -1),
            bfc2_terms.reshape(n, -1),
        ],
        axis=1,
    )
    wqkv_sum = add_up(exchange(wqkv_low, "chip")).astype(BF16)
    extra = as_rows(small_terms, sent_cols)
    got = exchange(jnp.concatenate([wqkv_sum, extra], axis=1), "narrow")
    got, grad_first, fc_all, last_terms = together(got, grad_first, fc_all, last_terms)
    grad_last = lax.psum_scatter(last_terms, "narrow", scatter_dimension=0, tiled=False)
    grad_wfc1, grad_wfc2 = call(
        functools.partial(unpack_kernel, n),
        (fc_all,),
        [((shard, n * w * hidden_dev), F32), ((w * hidden_dev, width), F32)],
        name="unpack",
        micros=8,
    )
    grad_first_all = jnp.concatenate([grad_first[: tokens // 2], grad_last]).astype(F32)
    grad_input = grad_middle + norm_back(unit_one, inv_one, grad_first_all * (1.0 + scale_one))

    small_own = jnp.sum(from_rows(got[:, padded:], small_terms.shape[1]), axis=0)
    wout_own = grad_first[tokens // 2 :]
    mod_size = mod_terms.shape[1]
    mod_low = small_own[:mod_size].astype(BF16)
    row = jnp.concatenate(
        [whole_lanes(small_own[:mod_size]), whole_lanes(cond_act[0]), small_own[mod_size:]]
    )
    small_rows = as_rows(row[None], sent_cols)[0]
    parts = -(-width // (sent_cols))
    half = jnp.concatenate(jnp.split(wout_own, parts, axis=1))
    half = jnp.pad(half, ((0, 0), (0, sent_cols - width // parts)))
    sent = jnp.concatenate(
        [
            got[:, :padded].reshape(n * padded, sent_cols),
            half,
            small_rows,
        ]
    )
    got_own = share(sent, "chip")
    cond_part = dot(mod_low[None], w_ada, ((1,), (1,)))
    cond_total = jnp.sum(ring_gather(cond_part), axis=0)
    got_own, grad_wfc1, cond_total = together(got_own, grad_wfc1, cond_total)
    got_other = flip(got_own, "core", 1)
    got_other, grad_input = together(got_other, grad_input)
    grad_wqkv, grad_wout, grad_wada, grad_bada, grad_qv, grad_bout, grad_bfc1, grad_bfc2 = call(
        functools.partial(finish_kernel, n, padded, cols),
        (core_at, got_own, got_other),
        [
            ((shard, 3 * width), F32),
            ((shard, width), F32),
            ((mod_size, width), F32),
            ((mod_size,), F32),
        ]
        + [(bias.shape, F32) for bias in (qv_bias, b_out, b_fc1, b_fc2)],
        [(got_own.shape, BF16)] * 2
        + [((w, small_rows.shape[0] // 2 * sent_cols), F32)]
        + [pltpu.SemaphoreType.DMA] * 2,
        scalars=1,
        space=pl.ANY,
        name="finish",
        micros=9,
    )
    grad_wada = grad_wada.T
    grad_condition = silu_pull(cond_total)[0]
    return (
        result[None],
        grad_input[None],
        grad_condition,
        grad_wada,
        grad_bada,
        grad_wqkv,
        grad_qv,
        grad_wout,
        grad_bout,
        grad_wfc1,
        grad_bfc1,
        grad_wfc2,
        grad_bfc2,
    )


def solution(mesh):
    narrow = mesh.shape["narrow"]
    mesh = Mesh(mesh.devices.reshape(-1, 2, narrow), ("chip", "core", "narrow"))
    in_specs = (
        P(WIDE, "narrow", None),
        P(WIDE, None),
        P(WIDE),
        P(None, "narrow"),
        P("narrow"),
        P("narrow", None),
        P("narrow"),
        P("narrow", None),
        P("narrow"),
        P("narrow", None),
        P("narrow"),
        P("narrow", None),
        P("narrow"),
        P(WIDE, "narrow", None),
    )
    out_specs = (
        P(WIDE, "narrow", None),
        P(WIDE, "narrow", None),
        P(WIDE, None),
        P(None, "narrow"),
        P("narrow"),
        P("narrow", None),
        P("narrow"),
        P("narrow", None),
        P("narrow"),
        P("narrow", None),
        P("narrow"),
        P("narrow", None),
        P("narrow"),
    )
    return jax.shard_map(
        per_device, mesh=mesh, in_specs=in_specs, out_specs=out_specs, check_vma=False
    )
```

```python
import functools
import math

import jax
import jax.numpy as jnp
from jax import lax
from jax.experimental import pallas as pl
from jax.experimental.pallas import tpu as pltpu
from jax.sharding import Mesh
from jax.sharding import PartitionSpec as P

HEADS = 16
WIDE = ("chip", "core")
F32 = jnp.float32
BF16 = jnp.bfloat16
LANES = 128
ROOT = math.sqrt(2 / math.pi)
LOG2E = math.log2(math.e)


def dot(left, right, dims=((1,), (0,))):
    return lax.dot_general(left, right, (dims, ((), ())), preferred_element_type=F32)


def flip(block, axis, bit):
    size = lax.axis_size(axis)
    return lax.ppermute(block, axis, [(i, i ^ bit) for i in range(size)])


def exchange(blocks, axis):
    return lax.all_to_all(blocks, axis, 0, 0, tiled=False)


def share(block, axis):
    return exchange(jnp.broadcast_to(block[None], (lax.axis_size(axis),) + block.shape), axis)


def ring(block, step):
    n = lax.axis_size("narrow")
    return lax.ppermute(block, "narrow", [(i, (i + step) % n) for i in range(n)])


def pick(blocks, index):
    return lax.dynamic_index_in_dim(blocks, index, 0, keepdims=False)


def together(*values):
    return lax.optimization_barrier(values)


def add_up(blocks):
    return sum(blocks[i].astype(F32) for i in range(blocks.shape[0]))


def place(blocks, index_of):
    buffer = jnp.zeros((len(blocks),) + blocks[0].shape, blocks[0].dtype)
    for j, block in enumerate(blocks):
        buffer = lax.dynamic_update_index_in_dim(buffer, block, index_of(j), 0)
    return buffer


def ring_gather(block):
    n = lax.axis_size("narrow")
    z = lax.axis_index("narrow")
    blocks = [block] + [ring(block, j) for j in range(1, n)]
    return place(blocks, lambda j: lax.rem(z + n - j, n))


def as_rows(values, columns):
    rows = -(-values.shape[1] // (4 * columns)) * 4
    values = jnp.pad(values, ((0, 0), (0, rows * columns - values.shape[1])))
    high = values.astype(BF16)
    low = (values - high.astype(F32)).astype(BF16)
    return jnp.concatenate([part.reshape(-1, rows, columns) for part in (high, low)], axis=1)


def from_rows(rows, size):
    half = rows.shape[1] // 2
    total = rows[:, :half].astype(F32) + rows[:, half:].astype(F32)
    return total.reshape(rows.shape[0], -1)[:, :size]


def whole_lanes(row):
    return jnp.pad(row, (0, -row.shape[0] % LANES))


def core_add(own, other):
    return (own.astype(F32) + flip(other, "core", 1).astype(F32)).astype(BF16)


def call(kernel, args, outs, scratch=(), scalars=0, name=None, micros=1, space=pltpu.VMEM):
    vmem = pl.BlockSpec(memory_space=pltpu.VMEM)
    given = pl.BlockSpec(memory_space=space)
    smem = pl.BlockSpec(memory_space=pltpu.SMEM)
    return pl.pallas_call(
        kernel,
        out_shape=tuple(jax.ShapeDtypeStruct(shape, dtype) for shape, dtype in outs),
        in_specs=[smem if i < scalars else given for i in range(len(args))],
        out_specs=tuple(vmem for _ in outs),
        scratch_shapes=[
            part if isinstance(part, pltpu.SemaphoreType) else pltpu.VMEM(*part) for part in scratch
        ],
        compiler_params=pltpu.CompilerParams(vmem_limit_bytes=56 << 20),
        cost_estimate=pl.CostEstimate(
            flops=1000000000 * micros, bytes_accessed=3000000 * micros, transcendentals=0
        ),
        name=name,
    )(*args)


def pack_kernel(n, w, p_ref, fc1_ref, fc2_ref, first_ref, second_ref):
    shard = fc1_ref.shape[0]
    rows = fc2_ref.shape[0] // w
    full = fc2_ref.shape[0]
    for q in range(w):

        @pl.when(p_ref[0] == q)
        def _(q=q):
            second_ref[...] = fc2_ref[q * rows : (q + 1) * rows]
            pieces = [
                fc1_ref[part : part + rows, a * full + q * rows : a * full + (q + 1) * rows]
                for part in range(0, shard, rows)
                for a in range(n)
            ]
            first_ref[...] = jnp.concatenate(pieces, axis=1)


def qkv_kernel(n, w, place_ref, w_ref, out_ref):
    padded, sent = out_ref.shape[1:]
    piece = w_ref.shape[0] // w
    width = w_ref.shape[1] // 3
    cols = width // n
    for q in range(w):

        @pl.when(place_ref[0] == q)
        def _(q=q):
            for a in range(n):
                block = jnp.concatenate(
                    [
                        w_ref[q * piece : (q + 1) * piece, t * width + a * cols : t * width + (a + 1) * cols]
                        for t in range(3)
                    ],
                    axis=1,
                )
                if sent > 3 * cols:
                    fill = jnp.zeros((piece, sent - 3 * cols), BF16)
                    block = jnp.concatenate([block, fill], axis=1)
                if padded > piece:
                    fill = jnp.zeros((padded - piece, sent), BF16)
                    block = jnp.concatenate([block, fill], axis=0)
                out_ref[a] = block


def qkv_join_kernel(n, heads, padded, core_ref, own_ref, other_ref, wide_ref, joined):
    chips = own_ref.shape[0]
    width = wide_ref.shape[0]
    piece = width // (n * 2 * chips)
    size = width // (n * heads)
    for core in range(2):

        @pl.when(core_ref[0] == core)
        def _(core=core):
            for q in range(2 * chips):
                got_ref = own_ref if q % 2 == core else other_ref
                for a in range(n):
                    at = (a * 2 * chips + q) * piece
                    joined[at : at + piece] = got_ref[q // 2, a * padded : a * padded + piece]

    pad = jnp.zeros((width, LANES - size), BF16)
    for t in range(3 * heads):
        wide_ref[:, t * LANES : (t + 1) * LANES] = jnp.concatenate(
            [joined[:, t * size : (t + 1) * size], pad], axis=1
        )


def attend_kernel(
    n, heads, scale, unit_ref, mod_ref, wide_ref, bias_ref, mixed_ref, proj_ref, lse_ref, mixed_wide
):
    width = unit_ref.shape[2]
    image = proj_ref.shape[0]
    tokens = image // n
    size = width // (n * heads)
    pad_row = jnp.zeros((1, LANES - size), F32)
    bias = []
    for t in range(3 * heads):
        bias += [bias_ref[:, t * size : (t + 1) * size], pad_row]
    bias = jnp.concatenate(bias, axis=1)
    gain = 1.0 + mod_ref[1:2]
    shift = mod_ref[0:1]

    def project(i, carry):
        rows = pl.ds(pl.multiple_of(i * 2 * tokens, 2 * tokens), 2 * tokens)
        both = jnp.concatenate([unit_ref[2 * i, :tokens], unit_ref[2 * i + 1, :tokens]], axis=0)
        first = (both.astype(F32) * gain + shift).astype(BF16)
        proj_ref[rows] = (dot(first, wide_ref[...]) + bias).astype(BF16)
        return carry

    lax.fori_loop(0, n // 2, project, 0)

    def head(h, carry):
        at = lambda t: pl.ds(pl.multiple_of((t * heads + h) * LANES, LANES), LANES)
        keys = proj_ref[:, at(1)]
        values_t = proj_ref[:, at(2)].T

        def block(i, carry):
            rows = pl.ds(pl.multiple_of(i * 4 * tokens, 4 * tokens), 4 * tokens)
            scores = dot(keys, proj_ref[rows, at(0)], ((1,), (1,)))
            top = jnp.max(scores, axis=0, keepdims=True)
            grown = jnp.exp2((scores - top) * (scale * LOG2E))
            total = jnp.sum(grown, axis=0, keepdims=True)
            mixed = dot(values_t, grown.astype(BF16)) / total
            mixed = mixed.T.astype(BF16)
            for k in range(4):
                mixed_wide[4 * i + k, h] = mixed[k * tokens : (k + 1) * tokens]
            lse_ref[h, :, rows] = top * (scale * LOG2E) + jnp.log2(total)
            return carry

        return lax.fori_loop(0, n // 4, block, carry)

    lax.fori_loop(0, heads, head, 0)

    def join(i, carry):
        rows = tokens // n
        mixed_ref[i] = jnp.concatenate(
            [
                mixed_wide[i, h, q * rows : (q + 1) * rows, :size]
                for q in range(n)
                for h in range(heads)
            ],
            axis=1,
        )
        return carry

    lax.fori_loop(0, n, join, 0)


def attend_back_kernel(
    n,
    heads,
    scale,
    core_ref,
    proj_ref,
    lse_ref,
    grad_ref,
    mixed_ref,
    unit_ref,
    mod_ref,
    wide_ref,
    *rest,
):
    terms_own_ref, terms_other_ref, first_ref, last_ref, sums_ref, proj_sums_ref = rest[:6]
    grad_proj, grad_wide, delta_ref, first_low, terms, query_acc, terms_low = rest[6:]
    width = unit_ref.shape[2]
    image = proj_ref.shape[0]
    tokens = image // n
    cols = grad_ref.shape[2] // n
    size = cols // heads
    pad = jnp.zeros((tokens, LANES - size), BF16)
    ones = jnp.ones((8, LANES), F32)
    gain = 1.0 + mod_ref[1:2]
    shift = mod_ref[0:1]

    def prepare(i, carry):
        rows = pl.ds(pl.multiple_of(i * tokens, tokens), tokens)
        for h in range(heads):
            lanes = [slice(q * cols + h * size, q * cols + (h + 1) * size) for q in range(n)]
            grad = jnp.concatenate([grad_ref[i, :, at] for at in lanes], axis=0)
            mixed = jnp.concatenate([mixed_ref[i, :, at] for at in lanes], axis=0)
            grad = jnp.concatenate([grad, pad], axis=1)
            mixed = jnp.concatenate([mixed, pad], axis=1)
            grad_wide[rows, h * LANES : (h + 1) * LANES] = grad
            both = grad.astype(F32) * mixed.astype(F32)
            delta = lax.dot_general(
                ones, both, (((1,), (1,)), ((), ())),
                preferred_element_type=F32, precision=lax.Precision.HIGHEST,
            )
            delta_ref[h, :, rows] = delta[0:1]
        first_low[rows] = (unit_ref[i, :tokens].astype(F32) * gain + shift).astype(BF16)
        return carry

    lax.fori_loop(0, n, prepare, 0)

    def head(h, carry):
        q_at, k_at, v_at = [
            pl.ds(pl.multiple_of((t * heads + h) * LANES, LANES), LANES) for t in range(3)
        ]
        query_acc[...] = jnp.zeros_like(query_acc)

        def block(j, carry):
            rows = pl.ds(pl.multiple_of(j * 4 * tokens, 4 * tokens), 4 * tokens)
            keys = proj_ref[rows, k_at]
            values = proj_ref[rows, v_at]
            queries = proj_ref[:, q_at]
            grads = grad_wide[:, q_at]
            weights = jnp.exp2(dot(keys, queries, ((1,), (1,))) * (scale * LOG2E) - lse_ref[h])
            grad_weights = dot(values, grads, ((1,), (1,)))
            grad_scores = (weights * (grad_weights - delta_ref[h])).astype(BF16)
            grad_proj[rows, v_at] = dot(weights.astype(BF16), grads).astype(BF16)
            grad_proj[rows, k_at] = (dot(grad_scores, queries) * scale).astype(BF16)
            query_acc[...] += dot(keys.T, grad_scores)
            return carry

        carry = lax.fori_loop(0, n // 4, block, carry)
        grad_proj[:, q_at] = (query_acc[...] * scale).T.astype(BF16)
        return carry

    lax.fori_loop(0, heads, head, 0)
    proj_sums_ref[...] = jnp.zeros_like(proj_sums_ref)
    sums_ref[...] = jnp.zeros_like(sums_ref)

    def out(i, carry):
        rows = pl.ds(pl.multiple_of(i * 2 * tokens, 2 * tokens), 2 * tokens)
        block = grad_proj[rows]
        grad = dot(block, wide_ref[...], ((1,), (1,)))
        proj_sums_ref[0:1] += jnp.sum(block.astype(F32), axis=0, keepdims=True)
        sums_ref[0:1] += jnp.sum(grad, axis=0, keepdims=True)
        for k in range(2):
            part = grad[k * tokens : (k + 1) * tokens]
            unit = unit_ref[2 * i + k, :tokens].astype(F32)
            sums_ref[1:2] += jnp.sum(part * unit, axis=0, keepdims=True)
            first_ref[2 * i + k] = part[: tokens // 2].astype(BF16)
            last_ref[2 * i + k] = part[tokens // 2 :].astype(BF16)
        return carry

    lax.fori_loop(0, n // 2, out, 0)

    def third(t, carry):
        lanes = pl.ds(pl.multiple_of(t * heads * LANES, LANES), heads * LANES)
        part = dot(first_low[...], grad_proj[:, lanes], ((0,), (0,)))
        terms[t] = jnp.concatenate(
            [part[:, h * LANES : h * LANES + size] for h in range(heads)], axis=1
        ).astype(BF16)
        return carry

    lax.fori_loop(0, 3, third, 0)
    _, chips, _, padded, sent = terms_low.shape

    def get(rows):
        parts = [terms[t, rows] for t in range(3)]
        if sent > 3 * cols:
            parts.append(jnp.zeros((parts[0].shape[0], sent - 3 * cols), BF16))
        return jnp.concatenate(parts, axis=1)

    def store(q, a, block):
        terms_low[q % 2, q // 2, a] = block

    to_pieces(get, store, n, width // n, 2 * chips, padded)
    terms_own_ref[...] = terms_low[core_ref[0]]
    terms_other_ref[...] = terms_low[1 - core_ref[0]]


def to_pieces(get, store, n, shard, w, padded):
    piece = shard // w
    for a in range(n):
        for q in range(w):
            at = a * shard + q * piece
            block = get(slice(at, at + piece))
            if padded > piece:
                fill = jnp.zeros((padded - piece, block.shape[1]), BF16)
                block = jnp.concatenate([block, fill], axis=0)
            store(q, a, block)


def out_join_kernel(n, core_ref, own_ref, other_ref, out_ref):
    chips = own_ref.shape[0]
    piece = out_ref.shape[0] // (n * 2 * chips)
    for core in range(2):

        @pl.when(core_ref[0] == core)
        def _(core=core):
            for q in range(2 * chips):
                part_ref = own_ref if q % 2 == core else other_ref
                for a in range(n):
                    at = (a * 2 * chips + q) * piece
                    out_ref[at : at + piece] = part_ref[q // 2, a, :piece]


def middle_kernel(
    n,
    got_ref,
    x_ref,
    mod_ref,
    bias_ref,
    out_ref,
    mixed_ref,
    branch_ref,
    middle_ref,
    second_ref,
):
    rows = got_ref.shape[1]
    cols = got_ref.shape[2] // n
    for q in range(n):
        mixed_ref[q * rows : (q + 1) * rows] = jnp.concatenate(
            [got_ref[j, :, q * cols : (q + 1) * cols] for j in range(n)], axis=1
        )
    branch = dot(mixed_ref[...], out_ref[...]) + bias_ref[...]
    middle = x_ref[...] + mod_ref[2:3] * branch
    unit, _ = norm_parts(middle)
    branch_ref[...] = branch
    middle_ref[...] = middle
    second = (unit * (1.0 + mod_ref[4:5]) + mod_ref[3:4]).astype(BF16)
    for k in range(second_ref.shape[0]):
        second_ref[k] = second


def middle_back_kernel(
    n, core_ref, came_ref, middle_ref, branch_ref, d_out_ref, mod_ref, out_ref, mixed_cat_ref, *rest
):
    grad_middle_ref, mixed_ref, sums_ref, own_ref, other_ref, grad_one_ref, terms, low = rest
    rows = mixed_ref.shape[1]
    cols = mixed_ref.shape[2] // n
    unit, inv = norm_parts(middle_ref[...])
    grad_second = came_ref[0].astype(F32)
    for r in range(1, came_ref.shape[0]):
        grad_second += came_ref[r].astype(F32)
    grad_middle = d_out_ref[...] + norm_back(unit, inv, grad_second * (1.0 + mod_ref[4:5]))
    grad_one = (mod_ref[2:3] * grad_middle).astype(BF16)
    grad_middle_ref[...] = grad_middle
    grad_one_ref[...] = grad_one
    parts = (grad_second, grad_second * unit, grad_middle * branch_ref[...], grad_one.astype(F32))
    for k, part in enumerate(parts):
        sums_ref[k : k + 1] = jnp.sum(part, axis=0, keepdims=True)
    mixed = dot(grad_one, out_ref[...], ((1,), (1,))).astype(BF16)
    for j in range(n):
        mixed_ref[j] = jnp.concatenate(
            [mixed[q * rows : (q + 1) * rows, j * cols : (j + 1) * cols] for q in range(n)], axis=1
        )
    step = grad_one_ref.shape[1] // 3

    def third(t, carry):
        lanes = pl.ds(pl.multiple_of(t * step, LANES), step)
        terms[:, lanes] = dot(mixed_cat_ref[...], grad_one_ref[:, lanes], ((0,), (0,))).astype(BF16)
        return carry

    lax.fori_loop(0, 3, third, 0)
    _, chips, _, padded, _ = low.shape

    def store(q, a, block):
        low[q % 2, q // 2, a] = block

    to_pieces(lambda rows: terms[rows], store, n, terms.shape[0] // n, 2 * chips, padded)
    for a in range(n):
        own_ref[:, a * padded : (a + 1) * padded] = low[core_ref[0], :, a]
        other_ref[:, a * padded : (a + 1) * padded] = low[1 - core_ref[0], :, a]


def mlp_kernel(
    n,
    own_ref,
    other_ref,
    two_own_ref,
    two_other_ref,
    pack_one_ref,
    pack_two_ref,
    bias_ref,
    second_own_ref,
    second_other_ref,
    two_sum_own_ref,
    two_sum_other_ref,
    grad_ref,
    bias_grad_ref,
    fc1,
    fc2,
    active_all,
    hidden_all,
    grad_fc1,
):
    chips, tokens, width = own_ref.shape
    rows = pack_one_ref.shape[1]
    units = n * rows
    halves = width // units
    for a in range(n):
        fc2[a * rows : (a + 1) * rows] = pack_two_ref[a]
        for part in range(halves):
            at = (a * halves + part) * rows
            fc1[at : at + rows] = pack_one_ref[a, :, part * units : (part + 1) * units]
    bias_grad_ref[...] = jnp.zeros_like(bias_grad_ref)
    sides = (
        (own_ref, two_own_ref, second_own_ref, two_sum_own_ref),
        (other_ref, two_other_ref, second_other_ref, two_sum_other_ref),
    )
    for side, refs in enumerate(sides):

        def block(i, carry, side=side, refs=refs):
            x_ref, g_ref, second_ref, two_ref = refs
            at = pl.ds(pl.multiple_of(side * chips * tokens + i * 2 * tokens, 2 * tokens), 2 * tokens)
            some = pl.ds(2 * i, 2)
            rows_x = x_ref[some].reshape(2 * tokens, width)
            rows_g = g_ref[some].reshape(2 * tokens, width)
            hidden = dot(rows_x, fc1[...]) + bias_ref[...]
            square = hidden * hidden
            inner = ROOT * (hidden + 0.044715 * square * hidden)
            bend = jnp.tanh(inner)
            half = 0.5 * (1.0 + bend)
            active = (hidden * half).astype(BF16)
            slope = half + 0.5 * hidden * (1.0 - bend * bend) * (ROOT * (1.0 + 3 * 0.044715 * square))
            grad = (dot(rows_g, fc2[...], ((1,), (1,))) * slope).astype(BF16)
            active_all[at] = active
            hidden_all[at] = grad
            second = dot(grad, fc1[...], ((1,), (1,))).astype(BF16)
            second_ref[some] = second.reshape(2, tokens, width)
            two_ref[some] = dot(active, fc2[...]).astype(BF16).reshape(2, tokens, width)
            bias_grad_ref[0:1] += jnp.sum(grad.astype(F32), axis=0, keepdims=True)
            return carry

        lax.fori_loop(0, chips // 2, block, 0)
    step = width // 3
    half_rows = chips * tokens

    def third(t, carry):
        lanes = pl.ds(pl.multiple_of(t * step, LANES), step)
        part = dot(
            active_all[:half_rows], two_own_ref[:, :, lanes].reshape(half_rows, step), ((0,), (0,))
        ) + dot(
            active_all[half_rows:], two_other_ref[:, :, lanes].reshape(half_rows, step), ((0,), (0,))
        )
        for a in range(n):
            grad_ref[a, :rows, lanes] = part[a * rows : (a + 1) * rows].astype(BF16)
        grad_fc1[lanes] = (
            dot(own_ref[:, :, lanes].reshape(half_rows, step), hidden_all[:half_rows], ((0,), (0,)))
            + dot(other_ref[:, :, lanes].reshape(half_rows, step), hidden_all[half_rows:], ((0,), (0,)))
        ).astype(BF16)
        return carry

    lax.fori_loop(0, 3, third, 0)
    for a in range(n):
        grad_ref[a, rows:] = jnp.concatenate(
            [
                grad_fc1[(a * halves + part) * rows : (a * halves + part + 1) * rows]
                for part in range(halves)
            ],
            axis=1,
        )


def unpack_kernel(n, got_ref, fc1_ref, fc2_ref):
    w, _, width = got_ref.shape
    rows = got_ref.shape[1] // 2
    units = n * rows
    full = w * rows
    for q in range(w):
        fc2_ref[q * rows : (q + 1) * rows] = got_ref[q, :rows].astype(F32)
    for part in range(width // units):
        for a in range(n):
            at = part * units + a * rows
            fc1_ref[part * rows : (part + 1) * rows, a * full : (a + 1) * full] = jnp.concatenate(
                [got_ref[q, rows:, at : at + rows].astype(F32) for q in range(w)], axis=1
            )


def finish_kernel(
    n,
    padded,
    cols,
    core_ref,
    own_from,
    other_from,
    wqkv_ref,
    wout_ref,
    wada_ref,
    bada_ref,
    *rest,
):
    bias_refs, (own_ref, other_ref, rows_ref, own_sem, other_sem) = rest[:-5], rest[-5:]
    own_copy = pltpu.make_async_copy(own_from, own_ref, own_sem)
    other_copy = pltpu.make_async_copy(other_from, other_ref, other_sem)
    own_copy.start()
    other_copy.start()
    own_copy.wait()
    other_copy.wait()
    chips, _, sent = own_ref.shape
    piece = wqkv_ref.shape[0] // (2 * chips)
    parts = -(-wout_ref.shape[1] // sent)
    part = wout_ref.shape[1] // parts
    base = (n + parts) * padded
    half = (own_ref.shape[1] - base) // 2
    for core in range(2):

        @pl.when(core_ref[0] == core)
        def _(core=core):
            for q in range(2 * chips):
                got_ref = own_ref if q % 2 == core else other_ref
                wqkv_ref[q * piece : (q + 1) * piece] = jnp.concatenate(
                    [
                        got_ref[q // 2, a * padded : a * padded + piece, t * cols : (t + 1) * cols]
                        .astype(F32)
                        for t in range(3)
                        for a in range(n)
                    ],
                    axis=1,
                )
                wout_ref[q * piece : (q + 1) * piece] = jnp.concatenate(
                    [
                        got_ref[q // 2, a * padded : a * padded + piece, :part].astype(F32)
                        for a in range(n, n + parts)
                    ],
                    axis=1,
                )
                small = got_ref[q // 2, base : base + half].astype(F32)
                small += got_ref[q // 2, base + half : base + 2 * half].astype(F32)
                rows_ref[q : q + 1] = jnp.concatenate(
                    [small[r : r + 1] for r in range(half)], axis=1
                )

    size, width = wada_ref.shape
    at = -(-size // LANES) * LANES
    mod = rows_ref[:, :size].astype(BF16)
    cond = rows_ref[:, at : at + width].astype(BF16)
    wada_ref[...] = dot(mod, cond, ((0,), (0,)))
    bada_ref[...] = jnp.sum(mod.astype(F32), axis=0)
    at += -(-width // LANES) * LANES
    for bias_ref in bias_refs:
        bias_ref[...] = jnp.sum(rows_ref[:, at : at + bias_ref.shape[0]], axis=0)
        at += bias_ref.shape[0]


def rows_mean(rows_in):
    return jnp.mean(rows_in, axis=-1, keepdims=True)


def norm_parts(rows_in):
    centered = rows_in - rows_mean(rows_in)
    inv = lax.rsqrt(rows_mean(centered * centered) + 1e-06)
    return centered * inv, inv


def norm_back(unit, inv, grad_unit):
    return inv * (grad_unit - rows_mean(grad_unit) - unit * rows_mean(grad_unit * unit))


def per_device(
    x_input,
    condition,
    counts,
    w_ada,
    b_ada,
    w_qkv,
    qv_bias,
    w_out,
    b_out,
    w_fc1,
    b_fc1,
    w_fc2,
    b_fc2,
    d_out,
):
    n = lax.axis_size("narrow")
    chips = lax.axis_size("chip")
    w = 2 * chips
    z = lax.axis_index("narrow")
    p = 2 * lax.axis_index("chip") + lax.axis_index("core")
    plane = ("chip", "core")
    slot_count, tokens, width = x_input.shape
    x_rows = x_input.reshape(tokens, width)
    heads = HEADS // n
    head_size = width // HEADS
    score_scale = head_size ** (-0.5)
    shard = width // n
    sub = shard // 4
    hidden_dev = w_fc2.shape[0] // w
    hidden_all = n * hidden_dev
    cols = heads * head_size
    image = n * tokens

    living = (counts[0] > 0).astype(F32)

    piece = shard // w
    padded = -(-piece // 8) * 8
    sent_cols = -(-3 * cols // LANES) * LANES
    wide_cols = 3 * heads * LANES
    core = lax.axis_index("core")
    core_at = jnp.asarray(core, jnp.int32).reshape(1)
    plane_at = jnp.asarray(p, jnp.int32).reshape(1)
    (qkv_to,) = call(
        functools.partial(qkv_kernel, n, w),
        (plane_at, w_qkv),
        [((n, padded, sent_cols), BF16)],
        scalars=1,
        name="qkv_to",
        micros=3,
    )
    qkv_got = exchange(qkv_to, "narrow").reshape(n * padded, sent_cols)
    qkv_own = share(qkv_got, "chip")
    (qkv_wide,) = call(
        functools.partial(qkv_join_kernel, n, heads, padded),
        (core_at, qkv_own, flip(qkv_own, "core", 1)),
        [((width, wide_cols), BF16)],
        [((width, sent_cols), BF16)],
        scalars=1,
        name="qkv_join",
        micros=4,
    )

    cond_act, silu_pull = jax.vjp(jax.nn.silu, condition)
    cond_low = cond_act.astype(BF16)
    x_rows, qkv_to = together(x_rows, qkv_to)
    unit_one, inv_one = norm_parts(x_rows)
    unit_low, cond_low = together(unit_one.astype(BF16), cond_low)
    out_mine = lax.dynamic_slice_in_dim(w_out, p * piece, piece, 0)
    out_mine = jnp.pad(out_mine, ((0, padded - piece), (0, 0)))
    unit_all = lax.all_gather(
        jnp.concatenate([unit_low, out_mine]), "narrow", axis=0, tiled=False
    )
    mod_part = dot(cond_low, w_ada)[0] + b_ada.astype(F32)
    small = jnp.concatenate([mod_part] + [v.astype(F32) for v in (qv_bias, b_out, b_fc1, b_fc2)])
    small_all = ring_gather(small)
    ends = [0]
    for piece in (mod_part, qv_bias, b_out, b_fc1, b_fc2):
        ends.append(ends[-1] + piece.shape[0])
    modulation, qv_full, bout_full, bfc1_full, bfc2_full = [
        small_all[:, low:high].reshape(-1) for low, high in zip(ends[:-1], ends[1:])
    ]
    shift_one, scale_one, gate_one, shift_two, scale_two, gate_two = [
        modulation[None, k * width : (k + 1) * width] for k in range(6)
    ]


    pack_one, pack_two = call(
        functools.partial(pack_kernel, n, w),
        (jnp.asarray(p, jnp.int32).reshape(1), w_fc1, w_fc2),
        [((hidden_dev, width), BF16)] * 2,
        scalars=1,
        name="pack",
        micros=3,
    )

    grad_out = living * d_out.reshape(tokens, width)
    grad_two = (gate_two * grad_out).astype(BF16)
    two_own = share(grad_two, "chip")
    unit_all, pack_one = together(unit_all, pack_one)
    out_own = share(unit_all[:, tokens:], "chip")
    pack_one = lax.all_gather(pack_one, "narrow", axis=0, tiled=False)
    bfc1_dev = lax.dynamic_index_in_dim(bfc1_full.reshape(n, w, hidden_dev), p, 1, keepdims=False)
    bfc1_dev = bfc1_dev.reshape(1, hidden_all)

    qv_two = qv_full.reshape(2, n, cols)
    q_bias = lax.dynamic_index_in_dim(qv_two[0], z, 0, keepdims=True)
    v_bias = lax.dynamic_index_in_dim(qv_two[1], z, 0, keepdims=True)
    bias_three = jnp.concatenate([q_bias, jnp.zeros_like(q_bias), v_bias], axis=1)
    mod_one = jnp.concatenate([shift_one, scale_one], axis=0)
    mixed, projected, lse = call(
        functools.partial(attend_kernel, n, heads, score_scale),
        (unit_all, mod_one, qkv_wide, bias_three),
        [
            ((n, tokens // n, width), BF16),
            ((image, wide_cols), BF16),
            ((heads, 1, image), F32),
        ],
        [((n, heads, tokens, LANES), BF16)],
        name="attend",
        micros=26,
    )
    mixed, two_own, out_own = together(mixed, two_own, out_own)
    two_other = flip(two_own, "core", 1)
    mixed_heads = mixed
    out_other = flip(out_own, "core", 1)
    mixed = exchange(mixed, "narrow")
    (out_all,) = call(
        functools.partial(out_join_kernel, n),
        (core_at, out_own, out_other),
        [((width, width), BF16)],
        scalars=1,
        name="out_join",
        micros=2,
    )
    mixed, out_all, pack_one, pack_two = together(mixed, out_all, pack_one, pack_two)
    pack_two = lax.all_gather(pack_two, "narrow", axis=0, tiled=False)

    mod_all = modulation.reshape(6, width)
    mixed_cat, branch_one, middle, second_low = call(
        functools.partial(middle_kernel, n),
        (mixed, x_rows, mod_all, bout_full[None], out_all),
        [
            ((tokens, width), BF16),
            ((tokens, width), F32),
            ((tokens, width), F32),
            ((chips, tokens, width), BF16),
        ],
        name="middle",
        micros=5,
    )

    second_own = exchange(second_low, "chip")
    second_own, pack_two = together(second_own, pack_two)
    second_other = flip(second_own, "core", 1)
    side = ((chips, tokens, width), BF16)
    second_terms_own, second_terms_other, two_terms_own, two_terms_other, fc_terms, bfc1_terms = call(
        functools.partial(mlp_kernel, n),
        (second_own, second_other, two_own, two_other, pack_one, pack_two, bfc1_dev),
        [side, side, side, side, ((n, 2 * hidden_dev, width), BF16), ((8, hidden_all), F32)],
        [
            ((width, hidden_all), BF16),
            ((hidden_all, width), BF16),
            ((w * tokens, hidden_all), BF16),
            ((w * tokens, hidden_all), BF16),
            ((width, hidden_all), BF16),
        ],
        name="mlp",
        micros=33,
    )
    bfc1_terms = bfc1_terms[0]
    fc_own = lax.psum_scatter(fc_terms, "narrow", scatter_dimension=0, tiled=False)
    second_got = exchange(core_add(second_terms_own, second_terms_other), "chip")
    chip = lax.axis_index("chip")
    two_came = flip(two_terms_other, "core", 1)
    two_sent = [
        (pick(two_terms_own, chip ^ r).astype(F32) + pick(two_came, chip ^ r).astype(F32)).astype(BF16)
        for r in range(chips)
    ]
    second_got, *two_sent = together(second_got, *two_sent)
    two_got = [two_sent[0]] + [flip(two_sent[r], "chip", r) for r in range(1, chips)]

    bfc2_terms = jnp.sum(grad_two.astype(F32), axis=0)

    grad_middle, grad_mixed, middle_sums, *wout_sides = call(
        functools.partial(middle_back_kernel, n),
        (core_at, second_got, middle, branch_one, grad_out, mod_all, out_all, mixed_cat),
        [((tokens, width), F32), ((n, tokens // n, width), BF16), ((4, width), F32)]
        + [((chips, n * padded, width), BF16)] * 2,
        [
            ((tokens, width), BF16),
            ((width, width), BF16),
            ((2, chips, n, padded, width), BF16),
        ],
        scalars=1,
        name="middle_back",
        micros=10,
    )
    grad_shift_two, grad_scale_two, grad_gate_one, bout_terms = middle_sums
    grad_mixed, fc_own = together(grad_mixed, fc_own)
    fc_all = lax.all_gather(fc_own, plane, axis=0, tiled=False)
    grad_mixed = exchange(grad_mixed, "narrow")
    grad_mixed, wout_low = together(grad_mixed, core_add(*wout_sides))
    wout_got = exchange(wout_low, "chip")

    wqkv_side = ((chips, n, padded, sent_cols), BF16)
    half_rows = ((n, tokens // 2, width), BF16)
    wqkv_own, wqkv_other, first_terms, last_terms, one_sums, projected_sums = call(
        functools.partial(attend_back_kernel, n, heads, score_scale),
        (core_at, projected, lse, grad_mixed, mixed_heads, unit_all, mod_one, qkv_wide),
        [wqkv_side, wqkv_side, half_rows, half_rows, ((8, width), F32), ((8, wide_cols), F32)],
        [
            ((image, wide_cols), BF16),
            ((image, heads * LANES), BF16),
            ((heads, 1, image), F32),
            ((image, width), BF16),
            ((3, width, cols), BF16),
            ((LANES, image), F32),
            ((2, chips, n, padded, sent_cols), BF16),
        ],
        name="attend_back",
        scalars=1,
        micros=38,
    )
    wqkv_own, wqkv_other, first_terms, fc_all, wout_got, *two_got = together(
        wqkv_own, wqkv_other, first_terms, fc_all, wout_got, *two_got
    )
    grad_shift_one = one_sums[0]
    grad_scale_one = one_sums[1]
    wout_sum = add_up(wout_got).astype(BF16).reshape(n, padded, width)
    first_terms = jnp.concatenate([first_terms, wout_sum], axis=1)
    grad_first = lax.psum_scatter(first_terms, "narrow", scatter_dimension=0, tiled=False)
    wqkv_low, *two_got = together(core_add(wqkv_own, wqkv_other), *two_got)
    branch_two = bfc2_full[None] + sum(term.astype(F32) for term in two_got)
    result = living * (middle + gate_two * branch_two)
    grad_gate_two = jnp.sum(grad_out * branch_two, axis=0)
    projected_sums = projected_sums[0].reshape(3, heads, LANES)[:, :, :head_size].reshape(3, cols)

    mod_terms = jnp.concatenate(
        [grad_shift_one, grad_scale_one, grad_gate_one, grad_shift_two, grad_scale_two, grad_gate_two]
    ).reshape(n, -1)
    qv_terms = jnp.zeros((2, n, cols), F32)
    qv_terms = lax.dynamic_update_slice(
        qv_terms, jnp.stack([projected_sums[0], projected_sums[2]])[:, None], (0, z, 0)
    )
    bfc1_wide = lax.dynamic_update_slice(
        jnp.zeros((n, w, hidden_dev), F32), bfc1_terms.reshape(n, 1, hidden_dev), (0, p, 0)
    )
    small_terms = jnp.concatenate(
        [
            mod_terms,
            qv_terms.reshape(n, -1),
            bout_terms.reshape(n, -1),
            bfc1_wide.reshape(n, -1),
            bfc2_terms.reshape(n, -1),
        ],
        axis=1,
    )
    wqkv_sum = add_up(exchange(wqkv_low, "chip")).astype(BF16)
    extra = as_rows(small_terms, sent_cols)
    got = exchange(jnp.concatenate([wqkv_sum, extra], axis=1), "narrow")
    got, grad_first, fc_all, last_terms = together(got, grad_first, fc_all, last_terms)
    grad_last = lax.psum_scatter(last_terms, "narrow", scatter_dimension=0, tiled=False)
    grad_wfc1, grad_wfc2 = call(
        functools.partial(unpack_kernel, n),
        (fc_all,),
        [((shard, n * w * hidden_dev), F32), ((w * hidden_dev, width), F32)],
        name="unpack",
        micros=8,
    )
    grad_first_all = jnp.concatenate([grad_first[: tokens // 2], grad_last]).astype(F32)
    grad_input = grad_middle + norm_back(unit_one, inv_one, grad_first_all * (1.0 + scale_one))

    small_own = jnp.sum(from_rows(got[:, padded:], small_terms.shape[1]), axis=0)
    wout_own = grad_first[tokens // 2 :]
    mod_size = mod_terms.shape[1]
    mod_low = small_own[:mod_size].astype(BF16)
    row = jnp.concatenate(
        [whole_lanes(small_own[:mod_size]), whole_lanes(cond_act[0]), small_own[mod_size:]]
    )
    small_rows = as_rows(row[None], sent_cols)[0]
    parts = -(-width // (sent_cols))
    half = jnp.concatenate(jnp.split(wout_own, parts, axis=1))
    half = jnp.pad(half, ((0, 0), (0, sent_cols - width // parts)))
    sent = jnp.concatenate(
        [
            got[:, :padded].reshape(n * padded, sent_cols),
            half,
            small_rows,
        ]
    )
    got_own = share(sent, "chip")
    cond_part = dot(mod_low[None], w_ada, ((1,), (1,)))
    cond_total = jnp.sum(ring_gather(cond_part), axis=0)
    got_own, grad_wfc1, cond_total = together(got_own, grad_wfc1, cond_total)
    got_other = flip(got_own, "core", 1)
    got_other, grad_input = together(got_other, grad_input)
    grad_wqkv, grad_wout, grad_wada, grad_bada, grad_qv, grad_bout, grad_bfc1, grad_bfc2 = call(
        functools.partial(finish_kernel, n, padded, cols),
        (core_at, got_own, got_other),
        [
            ((shard, 3 * width), F32),
            ((shard, width), F32),
            ((mod_size, width), F32),
            ((mod_size,), F32),
        ]
        + [(bias.shape, F32) for bias in (qv_bias, b_out, b_fc1, b_fc2)],
        [(got_own.shape, BF16)] * 2
        + [((w, small_rows.shape[0] // 2 * sent_cols), F32)]
        + [pltpu.SemaphoreType.DMA] * 2,
        scalars=1,
        space=pl.ANY,
        name="finish",
        micros=9,
    )
    grad_wada = grad_wada.T
    grad_condition = silu_pull(cond_total)[0]
    return (
        result[None],
        grad_input[None],
        grad_condition,
        grad_wada,
        grad_bada,
        grad_wqkv,
        grad_qv,
        grad_wout,
        grad_bout,
        grad_wfc1,
        grad_bfc1,
        grad_wfc2,
        grad_bfc2,
    )


def solution(mesh):
    narrow = mesh.shape["narrow"]
    mesh = Mesh(mesh.devices.reshape(-1, 2, narrow), ("chip", "core", "narrow"))
    in_specs = (
        P(WIDE, "narrow", None),
        P(WIDE, None),
        P(WIDE),
        P(None, "narrow"),
        P("narrow"),
        P("narrow", None),
        P("narrow"),
        P("narrow", None),
        P("narrow"),
        P("narrow", None),
        P("narrow"),
        P("narrow", None),
        P("narrow"),
        P(WIDE, "narrow", None),
    )
    out_specs = (
        P(WIDE, "narrow", None),
        P(WIDE, "narrow", None),
        P(WIDE, None),
        P(None, "narrow"),
        P("narrow"),
        P("narrow", None),
        P("narrow"),
        P("narrow", None),
        P("narrow"),
        P("narrow", None),
        P("narrow"),
        P("narrow", None),
        P("narrow"),
    )
    return jax.shard_map(
        per_device, mesh=mesh, in_specs=in_specs, out_specs=out_specs, check_vma=False
    )
```
